32 devices in a mesh: seq: 16 (over z, x, core), fsdp: 2 (over y).
Axes of the slice: x: 2, y: 2, z: 4, core: 2. Of those that a mesh axis runs over, the one named last changes fastest.
Arguments:
- activations: bfloat16 [65536, 2048], P('seq', 'fsdp'), may hold values from -3 to 3
- mix_first: bfloat16 [256, 256], replicated, may hold values from -0.375 to 0.375
- twiddle: float32 [256, 256], P('seq'), may hold values from 0.4 to 2
- mix_second: bfloat16 [256, 256], replicated, may hold values from -0.375 to 0.375
- up_first: bfloat16 [8, 256, 256], P('fsdp'), may hold values from -0.375 to 0.375
- up_second: bfloat16 [8, 256, 1024], P('fsdp'), may hold values from -0.375 to 0.375
- down_first: bfloat16 [8, 1024, 256], P('fsdp'), may hold values from -0.1875 to 0.1875
- down_second: bfloat16 [8, 256, 256], P('fsdp'), may hold values from -0.375 to 0.375
- grad_out: bfloat16 [65536, 2048], P('seq', 'fsdp'), may hold values from -3 to 3
Outputs:
- output: bfloat16 [65536, 2048], P('seq', 'fsdp')
- grad_inputs: bfloat16 [65536, 2048], P('seq', 'fsdp')
- grad_up_first: float32 [8, 256, 256], P('fsdp')
- grad_up_second: float32 [8, 256, 1024], P('fsdp')
- grad_down_first: float32 [8, 1024, 256], P('fsdp')
- grad_down_second: float32 [8, 256, 256], P('fsdp')
The draws below stay inside these ranges and needn't reach their ends.
All inputs are finite; a program needn't handle non-finite values.
Results may differ from the reference program's by a relative error of at most 0.01.
Values may be sent and summed in bfloat16 or wider, within the bound.
No kernel may reach another device: no remote copies, remote signals or barrier semaphores. Data moves between devices by JAX's collectives and lax.ppermute only.
A program may use at most 320 MiB of HBM per device.

```python
import math
import jax
import jax.numpy as jnp
from jax import lax

BLK = 256
D = 2048
FF = 8192
NBLK = 8
LENGTH = 65536


def shard_levels(key, extent, split, smallest, high):
    level, own = 1.0, jax.random.fold_in(key, 6)
    for dim, parts in split:
        heights = jnp.exp(jax.random.uniform(jax.random.fold_in(own, dim), (parts,), jnp.float32, smallest / len(split), high / len(split)))
        level = level * jnp.repeat(heights, extent[dim] // parts).reshape([-1 if axis == dim else 1 for axis in range(len(extent))])
    return level


def scatter_about(stream_key, shape, deviation, limit, pieces=(), kind=jnp.bfloat16):
    drawn = jax.random.normal(stream_key, shape, jnp.float32) * deviation
    if len(pieces) > 0:
        drawn = shard_levels(stream_key, shape, pieces, -0.22, 0.18) * drawn
    return jnp.clip(drawn, min=-limit, max=limit).astype(kind)


def setup_inputs(seed: int = 0) -> dict:
    key_of = jax.random.split(jax.random.key(seed), 10)
    activations = scatter_about(key_of[0], (LENGTH, D), 0.5, 3.0, ((0, 16), (1, 2)))
    mix_first = scatter_about(key_of[1], (BLK, BLK), BLK ** -0.5, 0.375)
    twiddle = jnp.clip(jnp.exp(math.log(2.0) - 1.609438 * jax.random.uniform(key_of[2], (BLK, BLK), jnp.float32) ** shard_levels(key_of[2], (BLK, BLK), ((0, 16),), -0.2, 0.2)), 0.4, 2.0)
    mix_second = scatter_about(key_of[3], (BLK, BLK), BLK ** -0.5, 0.375)
    up_first = scatter_about(key_of[4], (NBLK, D // NBLK, D // NBLK), (D // NBLK) ** -0.5, 0.375, ((0, 2),))
    up_second = scatter_about(key_of[5], (NBLK, D // NBLK, FF // NBLK), (D // NBLK) ** -0.5, 0.375, ((0, 2),))
    down_first = scatter_about(key_of[6], (NBLK, FF // NBLK, D // NBLK), (FF // NBLK) ** -0.5, 0.1875, ((0, 2),))
    down_second = scatter_about(key_of[7], (NBLK, D // NBLK, D // NBLK), (D // NBLK) ** -0.5, 0.375, ((0, 2),))
    grad_out = scatter_about(key_of[8], (LENGTH, D), 0.5, 3.0, ((0, 16), (1, 2)))
    return dict(activations=activations, mix_first=mix_first, twiddle=twiddle, mix_second=mix_second, up_first=up_first, up_second=up_second, down_first=down_first, down_second=down_second, grad_out=grad_out)


root_two_pi = 0.7978845608028654
cubic_term = 0.044715


def gelu_value(values):
    inner = root_two_pi * (values + cubic_term * values * values * values)
    return 0.5 * values * (1.0 + jnp.tanh(inner))


def gelu_slope(values):
    inner = root_two_pi * (values + cubic_term * values * values * values)
    hyper = jnp.tanh(inner)
    return 0.5 * (1.0 + hyper) + 0.5 * values * (1.0 - hyper * hyper) * root_two_pi * (1.0 + 3.0 * cubic_term * values * values)


def product(form, left, right):
    return jnp.einsum(form, left.astype(jnp.float32), right.astype(jnp.float32))


def permute_blocks(values):
    count, blocks, width = values.shape
    stride = width // blocks
    return jnp.transpose(values.reshape(count, blocks, blocks, stride), (0, 2, 3, 1)).reshape(count, blocks, width)


def unpermute_blocks(values):
    count, blocks, width = values.shape
    stride = width // blocks
    return jnp.transpose(values.reshape(count, blocks, stride, blocks), (0, 3, 1, 2)).reshape(count, blocks, width)


def mlp_block(hidden_rows, grad_rows, up_first, up_second, down_first, down_second):
    count = hidden_rows.shape[0]
    blocks, width = up_first.shape[0], up_first.shape[1]
    hidden_three = hidden_rows.reshape(count, blocks, width)
    up_mid = product("tkp,kpq->tkq", hidden_three, up_first).astype(jnp.bfloat16)
    up_perm = permute_blocks(up_mid)
    pre_act = product("tge,geo->tgo", up_perm, up_second)
    activated = gelu_value(pre_act).astype(jnp.bfloat16)
    down_mid = product("tgo,goq->tgq", activated, down_first).astype(jnp.bfloat16)
    down_perm = permute_blocks(down_mid)
    down_out = product("tge,geq->tgq", down_perm, down_second).reshape(count, blocks * width)
    output_rows = (hidden_rows.astype(jnp.float32) + down_out).astype(jnp.bfloat16)
    grad_three = grad_rows.reshape(count, blocks, width)
    sum_down_second = product("tge,tgq->geq", down_perm, grad_three)
    back_perm = product("tgq,geq->tge", grad_three, down_second).astype(jnp.bfloat16)
    back_mid = unpermute_blocks(back_perm)
    sum_down_first = product("tgo,tgq->goq", activated, back_mid)
    grad_act = product("tgq,goq->tgo", back_mid, down_first)
    grad_pre = (grad_act * gelu_slope(pre_act)).astype(jnp.bfloat16)
    sum_up_second = product("tge,tgo->geo", up_perm, grad_pre)
    grad_perm = product("tgo,geo->tge", grad_pre, up_second).astype(jnp.bfloat16)
    grad_mid = unpermute_blocks(grad_perm)
    sum_up_first = product("tkp,tkq->kpq", hidden_three, grad_mid)
    grad_inner = product("tkq,kpq->tkp", grad_mid, up_first).reshape(count, blocks * width)
    grad_hidden = (grad_rows.astype(jnp.float32) + grad_inner).astype(jnp.bfloat16)
    return output_rows, grad_hidden, (sum_up_first, sum_up_second, sum_down_first, sum_down_second)


def reference(activations, mix_first, twiddle, mix_second, up_first, up_second, down_first, down_second, grad_out):
    group = math.gcd(D, 128)
    count = D // group

    def split_groups(values):
        return jnp.moveaxis(values.reshape(BLK, BLK, count, group), 2, 0)

    def join_groups(values):
        return jnp.moveaxis(values, 0, 2).reshape(BLK * BLK, D)

    def forward_mix(portion):
        first_pass = (product("abc,bj->ajc", portion, mix_first) * twiddle[:, :, None]).astype(jnp.bfloat16)
        return product("ajc,ai->ijc", first_pass, mix_second).astype(jnp.bfloat16)

    mixed = join_groups(lax.map(forward_mix, split_groups(activations)))
    inputs_float = activations.astype(jnp.float32)
    gating = jax.nn.sigmoid(inputs_float)
    mixed_float = mixed.astype(jnp.float32)
    hidden = (inputs_float + gating * mixed_float).astype(jnp.bfloat16)

    rows_block = min(BLK * BLK, 2048)
    number = (BLK * BLK) // rows_block

    def scan_step(carry, inputs):
        output_rows, grad_rows, terms = mlp_block(inputs[0], inputs[1], up_first, up_second, down_first, down_second)
        carry = tuple(carry[index] + terms[index] for index in range(4))
        return carry, (output_rows, grad_rows)

    initial = (jnp.zeros(up_first.shape, jnp.float32), jnp.zeros(up_second.shape, jnp.float32),
               jnp.zeros(down_first.shape, jnp.float32), jnp.zeros(down_second.shape, jnp.float32))
    totals, stacked = lax.scan(scan_step, initial, (hidden.reshape(number, rows_block, D), grad_out.reshape(number, rows_block, D)))
    output = stacked[0].reshape(BLK * BLK, D)
    grad_hidden = stacked[1].reshape(BLK * BLK, D)
    grad_float = grad_hidden.astype(jnp.float32)
    grad_mixed = (grad_float * gating).astype(jnp.bfloat16)

    def backward_mix(portion):
        back_rows = product("ijc,ai->ajc", portion, mix_second).astype(jnp.bfloat16)
        twisted = (back_rows.astype(jnp.float32) * twiddle[:, :, None]).astype(jnp.bfloat16)
        return product("ajc,bj->abc", twisted, mix_first)

    mix_grad = join_groups(lax.map(backward_mix, split_groups(grad_mixed)))
    grad_inputs = (grad_float * (1.0 + gating * (1.0 - gating) * mixed_float) + mix_grad).astype(jnp.bfloat16)
    scale = 1.0 / BLK
    return (output, grad_inputs, totals[0] * scale, totals[1] * scale, totals[2] * scale, totals[3] * scale)
```

```python
import functools

import jax
import jax.numpy as jnp
from jax import lax
from jax.experimental import pallas as pl
from jax.experimental.pallas import tpu as pltpu
from jax.sharding import PartitionSpec as P


NBLK = 8
LANES = 128
CHUNKS = 4


root_two_pi = 0.7978845608028654
cubic_term = 0.044715

BF = jnp.bfloat16
F32 = jnp.float32


def gelu_value(values):
    inner = root_two_pi * (values + cubic_term * values * values * values)
    return 0.5 * values * (1.0 + jnp.tanh(inner))


def gelu_slope(values):
    inner = root_two_pi * (values + cubic_term * values * values * values)
    hyper = jnp.tanh(inner)
    return 0.5 * (1.0 + hyper) + 0.5 * values * (1.0 - hyper * hyper) * root_two_pi * (
        1.0 + 3.0 * cubic_term * values * values
    )


def product(form, left, right):
    return jnp.einsum(form, left, right, preferred_element_type=jnp.float32)


def column_pass(field, factor):
    result = product(
        "ajc,ai->ijc", lax.all_to_all(field, "seq", split_axis=1, concat_axis=0, tiled=True), factor
    ).astype(jnp.bfloat16)
    return lax.all_to_all(result, "seq", split_axis=0, concat_axis=1, tiled=True)


def shuffle_blocks(values):
    return lax.all_to_all(values, "fsdp", split_axis=2, concat_axis=1, tiled=True)


def spread_blocks(values):
    count, local_blocks, width = values.shape
    stride = width // NBLK
    received = shuffle_blocks(values)
    shaped = received.reshape(count, NBLK, local_blocks, stride)
    return jnp.transpose(shaped, (0, 2, 3, 1)).reshape(count, local_blocks, width)


def return_blocks(values):
    count, local_blocks, width = values.shape
    stride = width // NBLK
    parts = NBLK // local_blocks
    shaped = values.reshape(count, local_blocks, stride, parts, local_blocks)
    sending = jnp.transpose(shaped, (0, 1, 3, 4, 2)).reshape(count, local_blocks, width)
    received = shuffle_blocks(sending).reshape(count, NBLK, local_blocks, stride)
    return jnp.transpose(received, (0, 2, 1, 3)).reshape(count, local_blocks, width)


def blocks_layer(hidden, grad_out, up_first, up_second, down_first, down_second):
    count, channels = hidden.shape
    local_blocks, width = (up_first.shape[0], up_first.shape[1])
    hidden_three = hidden.reshape(count, local_blocks, width)
    up_mid = product("tkp,kpq->tkq", hidden_three, up_first).astype(jnp.bfloat16)
    up_perm = spread_blocks(up_mid)
    pre_act = product("tge,geo->tgo", up_perm, up_second)
    activated = gelu_value(pre_act).astype(jnp.bfloat16)
    down_mid = product("tgo,goq->tgq", activated, down_first).astype(jnp.bfloat16)
    down_perm = spread_blocks(down_mid)
    down_out = product("tge,geq->tgq", down_perm, down_second).reshape(count, channels)
    output = (hidden.astype(jnp.float32) + down_out).astype(jnp.bfloat16)
    grad_three = grad_out.reshape(count, local_blocks, width)
    sum_down_second = product("tge,tgq->geq", down_perm, grad_three)
    back_perm = product("tgq,geq->tge", grad_three, down_second).astype(jnp.bfloat16)
    back_mid = return_blocks(back_perm)
    sum_down_first = product("tgo,tgq->goq", activated, back_mid)
    grad_act = product("tgq,goq->tgo", back_mid, down_first)
    grad_pre = (grad_act * gelu_slope(pre_act)).astype(jnp.bfloat16)
    sum_up_second = product("tge,tgo->geo", up_perm, grad_pre)
    grad_perm = product("tgo,geo->tge", grad_pre, up_second).astype(jnp.bfloat16)
    grad_mid = return_blocks(grad_perm)
    sum_up_first = product("tkp,tkq->kpq", hidden_three, grad_mid)
    grad_inner = product("tkq,kpq->tkp", grad_mid, up_first).reshape(count, channels)
    grad_hidden = (grad_out.astype(jnp.float32) + grad_inner).astype(jnp.bfloat16)
    return (output, grad_hidden, (sum_up_first, sum_up_second, sum_down_first, sum_down_second))


def general_shards(
    activations,
    mix_first,
    twiddle,
    mix_second,
    up_first,
    up_second,
    down_first,
    down_second,
    grad_out,
):
    local_rows, local_channels = activations.shape
    block_rows = twiddle.shape[0]
    length = mix_first.shape[0]
    inputs_three = activations.reshape(block_rows, length, local_channels)
    first_pass = (product("abc,bj->ajc", inputs_three, mix_first) * twiddle[:, :, None]).astype(
        jnp.bfloat16
    )
    mixed = column_pass(first_pass, mix_second).reshape(local_rows, local_channels)
    inputs_float = activations.astype(jnp.float32)
    gating = jax.nn.sigmoid(inputs_float)
    mixed_float = mixed.astype(jnp.float32)
    hidden = (inputs_float + gating * mixed_float).astype(jnp.bfloat16)
    output, grad_hidden, grads = blocks_layer(
        hidden, grad_out, up_first, up_second, down_first, down_second
    )
    totals = lax.psum((grads[0], grads[1], grads[2], grads[3]), "seq")
    grad_float = grad_hidden.astype(jnp.float32)
    grad_mixed = (grad_float * gating).astype(jnp.bfloat16)
    back_rows = column_pass(grad_mixed.reshape(block_rows, length, local_channels), mix_second.T)
    twisted = (back_rows.astype(jnp.float32) * twiddle[:, :, None]).astype(jnp.bfloat16)
    mix_grad = product("ajc,bj->abc", twisted, mix_first).reshape(local_rows, local_channels)
    grad_inputs = (grad_float * (1.0 + gating * (1.0 - gating) * mixed_float) + mix_grad).astype(
        jnp.bfloat16
    )
    scale = 1.0 / length
    return (
        output,
        grad_inputs,
        totals[0] * scale,
        totals[1] * scale,
        totals[2] * scale,
        totals[3] * scale,
    )


def dot(left, right):
    return jnp.dot(left, right, preferred_element_type=F32)


def dot_nt(left, right):
    return lax.dot_general(left, right, (((1,), (1,)), ((), ())), preferred_element_type=F32)


def dot_tn(left, right):
    return lax.dot_general(left, right, (((0,), (0,)), ((), ())), preferred_element_type=F32)


def swap_rows(rows):
    size = rows * rows
    out = lax.broadcasted_iota(jnp.int32, (size, size), 0)
    inp = lax.broadcasted_iota(jnp.int32, (size, size), 1)
    same = (out // rows == inp % rows) & (out % rows == inp // rows)
    return jnp.where(same, 1.0, 0.0).astype(BF)


def swap_lanes(parts):
    lane = lax.broadcasted_iota(jnp.int32, parts[0].shape, 1)
    low = lane < 64
    even = (lane & 32) == 0
    x0, x1, x2, x3 = parts
    a0 = jnp.where(low, x0, pltpu.roll(x2, 64, 1))
    a2 = jnp.where(low, pltpu.roll(x0, 64, 1), x2)
    a1 = jnp.where(low, x1, pltpu.roll(x3, 64, 1))
    a3 = jnp.where(low, pltpu.roll(x1, 64, 1), x3)
    b0 = jnp.where(even, a0, pltpu.roll(a1, 32, 1))
    b1 = jnp.where(even, pltpu.roll(a0, 96, 1), a1)
    b2 = jnp.where(even, a2, pltpu.roll(a3, 32, 1))
    b3 = jnp.where(even, pltpu.roll(a2, 96, 1), a3)
    return b0, b1, b2, b3


def params(*semantics):
    return pltpu.CompilerParams(
        dimension_semantics=("arbitrary",) * len(semantics), vmem_limit_bytes=58 * 1024 * 1024
    )


def full(shape):
    zeros = (0,) * len(shape)
    return pl.BlockSpec(shape, lambda *_: zeros)


def first_kernel(chunks, span, rows, x_ref, w_ref, tw_ref, *rest):
    outs, scratch = rest[: len(chunks)], rest[len(chunks)]
    swap = swap_rows(rows)
    low, high = chunks[0] * span, (chunks[-1] + 1) * span
    weight = w_ref[...].T[low:high, :]
    scales = tw_ref[...].T[low:high, :]
    for a in range(rows):
        value = dot(weight, x_ref[a]) * scales[:, a : a + 1]
        scratch[a] = value.astype(BF)
    size = rows * rows
    for n, out in enumerate(outs):
        for group in range(span // rows):
            start = n * span + group * rows
            piece = scratch[:, start : start + rows, :].reshape(size, scratch.shape[2])
            out[group * size : (group + 1) * size, :] = dot(swap, piece).astype(BF)


def first_stage(chunks, x3, w1t, twt, cols=256):
    rows, length, channels = x3.shape
    span = length // CHUNKS
    shape = jax.ShapeDtypeStruct((span * rows, channels), BF)
    return pl.pallas_call(
        functools.partial(first_kernel, chunks, span, rows),
        grid=(channels // cols,),
        in_specs=[
            pl.BlockSpec((rows, length, cols), lambda c: (0, 0, c)),
            full(w1t.shape),
            full(twt.shape),
        ],
        out_specs=[pl.BlockSpec((span * rows, cols), lambda c: (0, c))] * len(chunks),
        out_shape=[shape] * len(chunks),
        scratch_shapes=[pltpu.VMEM((rows, span * len(chunks), cols), BF)],
        compiler_params=params(0),
        name="first",
    )(x3, w1t, twt)


def second_kernel(w_ref, x_ref, o_ref):
    seq, own, rows, cols = x_ref.shape
    weight = w_ref[...]
    for j in range(own):
        value = dot(weight, x_ref[:, j].reshape(seq * rows, cols))
        o_ref[:, j] = value.astype(BF).reshape(seq, rows, cols)


def second_stage(weight, field, seq, rows, cols=256):
    total, channels = field.shape
    own = total // (seq * rows)
    four = field.reshape(seq, own, rows, channels)
    spec = pl.BlockSpec((seq, own, rows, cols), lambda c: (0, 0, 0, c))
    out = pl.pallas_call(
        second_kernel,
        grid=(channels // cols,),
        in_specs=[full(weight.shape), spec],
        out_specs=spec,
        out_shape=jax.ShapeDtypeStruct(four.shape, BF),
        compiler_params=params(0),
        name="second",
    )(weight, four)
    return out.reshape(total, channels)


def spread_store(values, own_ref, send_ref):
    for half, ref in ((0, own_ref), (1, send_ref)):
        parts = [v[:, half * LANES : (half + 1) * LANES] for v in values]
        for g, part in enumerate(swap_lanes(parts)):
            ref[g] = part.astype(BF)


def gather_load(own_ref, recv_ref):
    own = swap_lanes([own_ref[g].astype(F32) for g in range(own_ref.shape[0])])
    recv = swap_lanes([recv_ref[g].astype(F32) for g in range(recv_ref.shape[0])])
    return [jnp.concatenate([a, b], axis=1).astype(BF) for a, b in zip(own, recv)]


def back_kernel(g_ref, w_ref, own_ref, send_ref):
    rows, cols, channels = g_ref.shape
    grad = g_ref[...].reshape(rows * cols, channels)
    blocks, width = w_ref.shape[0], w_ref.shape[2]
    values = [dot_nt(grad[:, h * width : (h + 1) * width], w_ref[h]) for h in range(blocks)]
    spread_store(values, own_ref, send_ref)


def back_stage(chunk, g3, down_second):
    rows, length, channels = g3.shape
    size = rows * rows
    steps = length // CHUNKS // rows
    blocks = down_second.shape[0]
    shape = jax.ShapeDtypeStruct((blocks, steps * size, LANES), BF)
    spec = pl.BlockSpec((blocks, size, LANES), lambda s: (0, s, 0))
    return pl.pallas_call(
        back_kernel,
        grid=(steps,),
        in_specs=[
            pl.BlockSpec((rows, rows, channels), lambda s: (0, chunk * steps + s, 0)),
            full(down_second.shape),
        ],
        out_specs=[spec, spec],
        out_shape=[shape, shape],
        compiler_params=params(0),
        name="back",
    )(g3, down_second)


def hidden_kernel(x_ref, m_ref, w_ref, h_ref, own_ref, send_ref):
    rows, cols, channels = x_ref.shape
    mixed = dot(swap_rows(rows), m_ref[...])
    inputs = x_ref[...].reshape(rows * cols, channels).astype(F32)
    hidden = (inputs + jax.nn.sigmoid(inputs) * mixed).astype(BF)
    h_ref[...] = hidden
    blocks, width = w_ref.shape[0], w_ref.shape[1]
    values = [dot(hidden[:, k * width : (k + 1) * width], w_ref[k]) for k in range(blocks)]
    spread_store(values, own_ref, send_ref)


def hidden_stage(chunk, x3, mixed, up_first):
    rows, length, channels = x3.shape
    size = rows * rows
    steps = length // CHUNKS // rows
    blocks = up_first.shape[0]
    flat = pl.BlockSpec((size, channels), lambda s: (s, 0))
    part = pl.BlockSpec((blocks, size, LANES), lambda s: (0, s, 0))
    return pl.pallas_call(
        hidden_kernel,
        grid=(steps,),
        in_specs=[
            pl.BlockSpec((rows, rows, channels), lambda s: (0, chunk * steps + s, 0)),
            flat,
            full(up_first.shape),
        ],
        out_specs=[flat, part, part],
        out_shape=[
            jax.ShapeDtypeStruct(mixed.shape, BF),
            jax.ShapeDtypeStruct((blocks, mixed.shape[0], LANES), BF),
            jax.ShapeDtypeStruct((blocks, mixed.shape[0], LANES), BF),
        ],
        compiler_params=params(0),
        name="hidden",
    )(x3, mixed, up_first)


def middle_kernel(fresh, cols, *refs):
    uo, ur, bo, br, us, df = refs[:6]
    refs = refs[6:]
    if not fresh:
        sus_in, sdf_in = refs[:2]
        refs = refs[2:]
    down_own, down_send, grad_own, grad_send, sus, sdf = refs
    start = pl.program_id(1) == 0

    @pl.when(start)
    def _():
        if fresh:
            sus[...] = jnp.zeros(sus.shape, F32)
            sdf[...] = jnp.zeros(sdf.shape, F32)
        else:
            sus[...] = sus_in[...]
            sdf[...] = sdf_in[...]

    up = jnp.concatenate([uo[0], ur[0]], axis=1)
    back = jnp.concatenate([bo[0], br[0]], axis=1)
    hidden_units = us.shape[2]
    down = None
    grad = None
    for low in range(0, hidden_units, cols):
        part = slice(low, low + cols)
        z = dot(up, us[0, :, part])
        z2 = z * z
        h = 0.5 + 0.5 * jnp.tanh(z * (root_two_pi + (root_two_pi * cubic_term) * z2))
        act = (z * h).astype(BF)
        slope = h + (h - h * h) * (
            z * (2.0 * root_two_pi + (6.0 * root_two_pi * cubic_term) * z2)
        )
        pre = (dot_nt(back, df[0, part, :]) * slope).astype(BF)
        step = dot(act, df[0, part, :])
        down = step if down is None else down + step
        step = dot_nt(pre, us[0, :, part])
        grad = step if grad is None else grad + step
        sdf[0, part, :] += dot_tn(act, back)
        sus[0, :, part] += dot_tn(up, pre)
    down_own[0] = down[:, :LANES].astype(BF)
    down_send[0] = down[:, LANES:].astype(BF)
    grad_own[0] = grad[:, :LANES].astype(BF)
    grad_send[0] = grad[:, LANES:].astype(BF)


def middle_stage(up_own, up_recv, back_own, back_recv, up_second, down_first, sums, tile=512, cols=256):
    blocks, count, _ = up_own.shape
    steps = count // tile
    part = pl.BlockSpec((1, tile, LANES), lambda g, t: (g, t, 0))
    us_spec = pl.BlockSpec((1,) + up_second.shape[1:], lambda g, t: (g, 0, 0))
    df_spec = pl.BlockSpec((1,) + down_first.shape[1:], lambda g, t: (g, 0, 0))
    fresh = sums is None
    shape = jax.ShapeDtypeStruct(up_own.shape, BF)
    return pl.pallas_call(
        functools.partial(middle_kernel, fresh, cols),
        grid=(blocks, steps),
        in_specs=[part, part, part, part, us_spec, df_spec] + ([] if fresh else [us_spec, df_spec]),
        out_specs=[part] * 4 + [us_spec, df_spec],
        out_shape=[shape] * 4
        + [jax.ShapeDtypeStruct(up_second.shape, F32), jax.ShapeDtypeStruct(down_first.shape, F32)],
        input_output_aliases={} if fresh else {6: 4, 7: 5},
        compiler_params=params(0, 0),
        name="middle",
    )(up_own, up_recv, back_own, back_recv, up_second, down_first, *(() if fresh else sums))


def input_kernel(fresh, *refs):
    x_ref, g_ref, m_ref, h_ref, go, gr, w_ref = refs[:7]
    refs = refs[7:]
    if not fresh:
        suf_in = refs[0]
        refs = refs[1:]
    send_ref, base_ref, suf = refs

    @pl.when(pl.program_id(0) == 0)
    def _():
        suf[...] = jnp.zeros(suf.shape, F32) if fresh else suf_in[...]

    rows, cols, channels = x_ref.shape
    size = rows * cols
    swap = swap_rows(rows)
    width = w_ref.shape[1]
    mids = gather_load(go, gr)
    x3, g3 = x_ref[...].reshape(size, channels), g_ref[...].reshape(size, channels)
    for k, mid in enumerate(mids):
        part = slice(k * width, (k + 1) * width)
        inner = dot_nt(mid, w_ref[k])
        suf[k] += dot_tn(h_ref[:, part], mid)
        grad = (g3[:, part].astype(F32) + inner).astype(BF).astype(F32)
        gating = jax.nn.sigmoid(x3[:, part].astype(F32))
        mixed = dot(swap, m_ref[:, part])
        send_ref[:, part] = dot(swap, (grad * gating).astype(BF)).astype(BF)
        base_ref[:, part] = (grad * (1.0 + gating * (1.0 - gating) * mixed)).astype(BF)


def input_stage(chunk, x3, g3, mixed, hidden, grad_own, grad_recv, up_first, sums):
    rows, length, channels = x3.shape
    size = rows * rows
    steps = length // CHUNKS // rows
    blocks = up_first.shape[0]
    natural = pl.BlockSpec((rows, rows, channels), lambda s: (0, chunk * steps + s, 0))
    flat = pl.BlockSpec((size, channels), lambda s: (s, 0))
    part = pl.BlockSpec((blocks, size, LANES), lambda s: (0, s, 0))
    fresh = sums is None
    wspec = full(up_first.shape)
    return pl.pallas_call(
        functools.partial(input_kernel, fresh),
        grid=(steps,),
        in_specs=[natural, natural, flat, flat, part, part, wspec] + ([] if fresh else [wspec]),
        out_specs=[flat, flat, wspec],
        out_shape=[
            jax.ShapeDtypeStruct(mixed.shape, BF),
            jax.ShapeDtypeStruct(mixed.shape, BF),
            jax.ShapeDtypeStruct(up_first.shape, F32),
        ],
        input_output_aliases={} if fresh else {7: 2},
        compiler_params=params(0),
        name="inputs",
    )(x3, g3, mixed, hidden, grad_own, grad_recv, up_first, *(() if fresh else (sums,)))


def output_kernel(fresh, *refs):
    g_ref, h_ref, do, dr, w_ref = refs[:5]
    refs = refs[5:]
    if not fresh:
        sds_in = refs[0]
        refs = refs[2:]
    o_ref, sds = refs

    @pl.when(pl.program_id(0) == 0)
    def _():
        sds[...] = jnp.zeros(sds.shape, F32) if fresh else sds_in[...]

    rows, cols, channels = g_ref.shape
    size = rows * cols
    width = w_ref.shape[2]
    g3 = g_ref[...].reshape(size, channels)
    for h, perm in enumerate(gather_load(do, dr)):
        part = slice(h * width, (h + 1) * width)
        value = h_ref[:, part].astype(F32) + dot(perm, w_ref[h])
        o_ref[:, :, part] = value.astype(BF).reshape(rows, cols, width)
        sds[h] += dot_tn(perm, g3[:, part])


def output_stage(chunk, g3, hidden, down_own, down_recv, down_second, sums, output):
    rows, length, channels = g3.shape
    size = rows * rows
    steps = length // CHUNKS // rows
    blocks = down_second.shape[0]
    natural = pl.BlockSpec((rows, rows, channels), lambda s: (0, chunk * steps + s, 0))
    flat = pl.BlockSpec((size, channels), lambda s: (s, 0))
    part = pl.BlockSpec((blocks, size, LANES), lambda s: (0, s, 0))
    fresh = sums is None
    wspec = full(down_second.shape)
    return pl.pallas_call(
        functools.partial(output_kernel, fresh),
        grid=(steps,),
        in_specs=[natural, flat, part, part, wspec]
        + ([] if fresh else [wspec, pl.BlockSpec(memory_space=pl.ANY)]),
        out_specs=[natural, wspec],
        out_shape=[
            jax.ShapeDtypeStruct(g3.shape, BF),
            jax.ShapeDtypeStruct(down_second.shape, F32),
        ],
        input_output_aliases={} if fresh else {5: 1, 6: 0},
        compiler_params=params(0),
        name="outputs",
    )(g3, hidden, down_own, down_recv, down_second, *(() if fresh else (sums, output)))


def last_kernel(rows, w_ref, tw_ref, *refs):
    chunk_refs, base_refs = refs[:CHUNKS], refs[CHUNKS : 2 * CHUNKS]
    o_ref, scratch = refs[2 * CHUNKS :]
    size = rows * rows
    swap = swap_rows(rows)
    cols = o_ref.shape[2]
    groups = chunk_refs[0].shape[0] // size
    for n, ref in enumerate(chunk_refs):
        for g in range(groups):
            index = n * groups + g
            value = dot(swap, ref[g * size : (g + 1) * size, :]) * tw_ref[:, index : index + 1]
            scratch[:, index * rows : (index + 1) * rows, :] = value.astype(BF).reshape(rows, rows, cols)
    weight = w_ref[...]
    for a in range(rows):
        base = jnp.concatenate(
            [ref[g * size + a * rows : g * size + (a + 1) * rows, :] for ref in base_refs for g in range(groups)],
            axis=0,
        )
        o_ref[a] = (dot(weight, scratch[a]) + base.astype(F32)).astype(BF)


def last_stage(rows, length, mix_first, tw_cols, fields, bases, cols=256):
    channels = fields[0].shape[1]
    spec = pl.BlockSpec((fields[0].shape[0], cols), lambda c: (0, c))
    return pl.pallas_call(
        functools.partial(last_kernel, rows),
        grid=(channels // cols,),
        in_specs=[full(mix_first.shape), full(tw_cols.shape)] + [spec] * (2 * CHUNKS),
        out_specs=pl.BlockSpec((rows, length, cols), lambda c: (0, 0, c)),
        out_shape=jax.ShapeDtypeStruct((rows, length, channels), BF),
        scratch_shapes=[pltpu.VMEM((rows, length, cols), BF)],
        compiler_params=params(0),
        name="last",
    )(mix_first, tw_cols, *fields, *bases)


def exchange(field):
    return lax.all_to_all(field, "seq", split_axis=0, concat_axis=0, tiled=True)


def partner(values):
    return lax.ppermute(values, "fsdp", [(0, 1), (1, 0)])


PLAN = (
    (1, 0, (("first", 1), ("back", 0), ("back", 1), ("back", 2), ("back", 3))),
    (1, 1, (("second", 0),)),
    (2, 0, (("second", 1),)),
    (1, 2, (("hidden", 0),)),
    (2, 1, (("second", 2), ("middle", 0))),
    (1, 3, (("hidden", 1), ("inputs", 0))),
    (2, 2, (("second", 3), ("middle", 1))),
    (2, 3, (("hidden", 2), ("inputs", 1), ("outputs", 0))),
    (3, 0, (("hidden", 3), ("middle", 2))),
    (3, 1, (("fourth", 0), ("middle", 3), ("inputs", 2))),
    (4, 0, (("fourth", 1), ("outputs", 1), ("inputs", 3))),
    (3, 2, (("outputs", 2), ("outputs", 3), ("scatter", 0))),
    (4, 1, (("fourth", 2),)),
    (3, 3, (("across", 0),)),
    (4, 2, (("fourth", 3), ("gather", 0))),
    (4, 3, (("finish", 0),)),
)


def tie(value, others):
    return lax.optimization_barrier((value, others))[0]


def chunked_shards(
    seq,
    activations,
    mix_first,
    twiddle,
    mix_second,
    up_first,
    up_second,
    down_first,
    down_second,
    grad_out,
):
    local_rows, channels = activations.shape
    rows, length = twiddle.shape
    blocks, width = up_first.shape[0], up_first.shape[1]
    stride = width // NBLK
    mine = lax.axis_index("fsdp")

    def own_first(values, axis):
        return jnp.where(mine == 0, values, jnp.roll(values, LANES, axis))

    def group_rows(weight):
        shaped = weight.reshape(blocks, stride, NBLK, weight.shape[2])
        return own_first(jnp.transpose(shaped, (0, 2, 1, 3)).reshape(weight.shape), 1)

    def ungroup_rows(weight):
        shaped = own_first(weight, 1).reshape(blocks, NBLK, stride, weight.shape[2])
        return jnp.transpose(shaped, (0, 2, 1, 3)).reshape(weight.shape)

    x3 = activations.reshape(rows, length, channels)
    g3 = grad_out.reshape(rows, length, channels)
    w2, w2t = mix_second, mix_second.T
    ups_first, downs_first = own_first(up_first, 2), own_first(down_first, 2)
    ups_second, downs_second = group_rows(up_second), group_rows(down_second)
    tw_cols = jnp.transpose(twiddle.reshape(rows, length // rows, rows), (0, 2, 1)).reshape(
        rows * rows, length // rows
    )

    sends = first_stage((0,), x3, mix_first, twiddle)
    going = {(1, 0): sends[0]}
    arrived, kept = {}, {}
    sums, sum_first, sum_last, output = None, None, None, None
    last = sends[0]
    done = sends[0]

    half = seq // 2
    halves = [list(range(half)), list(range(half, seq))]
    across = [(d, (d + half) % seq) for d in range(seq)]

    for step, chunk_of_step, tasks in PLAN:
        previous = done
        done = exchange(tie(going[step, chunk_of_step], (last, previous)))
        arrived[step, chunk_of_step] = done
        last = previous
        for name, n in tasks:
            if name == "first":
                results = first_stage(tuple(range(1, CHUNKS)), tie(x3, last), mix_first, twiddle)
                for m, sent in enumerate(results):
                    going[1, m + 1] = sent
                last = results[0]
            elif name == "back":
                own, send = back_stage(n, tie(g3, last), downs_second)
                kept["back", n] = (own, partner(send))
                last = own
            elif name == "second":
                last = going[2, n] = second_stage(w2t, tie(arrived[1, n], last), seq, rows)
            elif name == "hidden":
                hidden, own, send = hidden_stage(n, x3, tie(arrived[2, n], last), ups_first)
                kept["hidden", n] = hidden
                kept["up", n] = (own, partner(send))
                last = own
            elif name == "middle":
                up_own, up_recv = kept["up", n]
                back_own, back_recv = kept["back", n]
                down_own, down_send, grad_own, grad_send, *sums = middle_stage(
                    tie(up_own, last), up_recv, back_own, back_recv, ups_second, downs_first, sums
                )
                kept["grad", n] = (grad_own, partner(grad_send))
                kept["down", n] = (down_own, partner(down_send))
                last = down_own
            elif name == "inputs":
                going[3, n], kept["base", n], sum_first = input_stage(
                    n,
                    x3,
                    g3,
                    arrived[2, n],
                    kept["hidden", n],
                    tie(kept["grad", n][0], last),
                    kept["grad", n][1],
                    ups_first,
                    sum_first,
                )
                last = going[3, n]
            elif name == "outputs":
                output, sum_last = output_stage(
                    n,
                    g3,
                    kept["hidden", n],
                    tie(kept["down", n][0], last),
                    kept["down", n][1],
                    downs_second,
                    sum_last,
                    output,
                )
                last = sum_last
            elif name == "scatter":
                count = sums[0].shape[0] * sums[0].shape[1]
                parts = (
                    sums[0].reshape(count, -1),
                    jnp.concatenate([v.reshape(-1, width) for v in (sums[1], sum_first, sum_last)], axis=0),
                )
                parts = [
                    lax.psum_scatter(v, "seq", scatter_dimension=0, axis_index_groups=halves, tiled=True)
                    for v in parts
                ]
            elif name == "across":
                parts = [(tie(v, last) * (1.0 / length)).astype(BF) for v in parts]
                others = [lax.ppermute(v, "seq", across) for v in parts]
                last = parts
            elif name == "gather":
                parts = [
                    (v.astype(F32) + tie(w, last).astype(F32)).astype(BF) for v, w in zip(parts, others)
                ]
                wholes = [
                    lax.all_gather(v, "seq", axis=0, axis_index_groups=halves, tiled=True) for v in parts
                ]
                last = parts
            elif name == "finish":
                one, two = tie(wholes, last)
                rest = two.reshape(-1, width, width)
                cut = down_first.shape[0] * down_first.shape[1] // width
                grads = (
                    own_first(rest[cut : cut + blocks].astype(F32), 2),
                    ungroup_rows(one.astype(F32).reshape(up_second.shape)),
                    own_first(rest[:cut].astype(F32).reshape(down_first.shape), 2),
                    ungroup_rows(rest[cut + blocks :].astype(F32)),
                )
            else:
                last = going[4, n] = second_stage(w2, tie(arrived[3, n], last), seq, rows)

    fields = [arrived[4, n] for n in range(CHUNKS)]
    bases = [kept["base", n] for n in range(CHUNKS)]
    grad_inputs = last_stage(rows, length, mix_first, tw_cols, fields, bases)
    return (
        output.reshape(local_rows, channels),
        grad_inputs.reshape(local_rows, channels),
        *grads,
    )


def shards(*args):
    _, _, twiddle, _, up_first = args[:5]
    rows, length = twiddle.shape
    blocks, width = up_first.shape[0], up_first.shape[1]
    seq = length // rows
    fits = (
        blocks * (width // NBLK) == LANES
        and 2 * blocks == NBLK
        and rows == 16
        and seq == 16
        and length % (CHUNKS * seq) == 0
    )
    if fits:
        return chunked_shards(seq, *args)
    return general_shards(*args)


def solution(mesh):
    in_specs = (
        P("seq", "fsdp"),
        P(),
        P("seq", None),
        P(),
        P("fsdp", None, None),
        P("fsdp", None, None),
        P("fsdp", None, None),
        P("fsdp", None, None),
        P("seq", "fsdp"),
    )
    out_specs = (
        P("seq", "fsdp"),
        P("seq", "fsdp"),
        P("fsdp", None, None),
        P("fsdp", None, None),
        P("fsdp", None, None),
        P("fsdp", None, None),
    )
    return jax.shard_map(shards, mesh=mesh, in_specs=in_specs, out_specs=out_specs, check_vma=False)
```

```python
import functools

import jax
import jax.numpy as jnp
from jax import lax
from jax.experimental import pallas as pl
from jax.experimental.pallas import tpu as pltpu
from jax.sharding import PartitionSpec as P


NBLK = 8
LANES = 128
CHUNKS = 4


root_two_pi = 0.7978845608028654
cubic_term = 0.044715

BF = jnp.bfloat16
F32 = jnp.float32


def gelu_value(values):
    inner = root_two_pi * (values + cubic_term * values * values * values)
    return 0.5 * values * (1.0 + jnp.tanh(inner))


def gelu_slope(values):
    inner = root_two_pi * (values + cubic_term * values * values * values)
    hyper = jnp.tanh(inner)
    return 0.5 * (1.0 + hyper) + 0.5 * values * (1.0 - hyper * hyper) * root_two_pi * (
        1.0 + 3.0 * cubic_term * values * values
    )


def product(form, left, right):
    return jnp.einsum(form, left, right, preferred_element_type=jnp.float32)


def column_pass(field, factor):
    result = product(
        "ajc,ai->ijc", lax.all_to_all(field, "seq", split_axis=1, concat_axis=0, tiled=True), factor
    ).astype(jnp.bfloat16)
    return lax.all_to_all(result, "seq", split_axis=0, concat_axis=1, tiled=True)


def shuffle_blocks(values):
    return lax.all_to_all(values, "fsdp", split_axis=2, concat_axis=1, tiled=True)


def spread_blocks(values):
    count, local_blocks, width = values.shape
    stride = width // NBLK
    received = shuffle_blocks(values)
    shaped = received.reshape(count, NBLK, local_blocks, stride)
    return jnp.transpose(shaped, (0, 2, 3, 1)).reshape(count, local_blocks, width)


def return_blocks(values):
    count, local_blocks, width = values.shape
    stride = width // NBLK
    parts = NBLK // local_blocks
    shaped = values.reshape(count, local_blocks, stride, parts, local_blocks)
    sending = jnp.transpose(shaped, (0, 1, 3, 4, 2)).reshape(count, local_blocks, width)
    received = shuffle_blocks(sending).reshape(count, NBLK, local_blocks, stride)
    return jnp.transpose(received, (0, 2, 1, 3)).reshape(count, local_blocks, width)


def blocks_layer(hidden, grad_out, up_first, up_second, down_first, down_second):
    count, channels = hidden.shape
    local_blocks, width = (up_first.shape[0], up_first.shape[1])
    hidden_three = hidden.reshape(count, local_blocks, width)
    up_mid = product("tkp,kpq->tkq", hidden_three, up_first).astype(jnp.bfloat16)
    up_perm = spread_blocks(up_mid)
    pre_act = product("tge,geo->tgo", up_perm, up_second)
    activated = gelu_value(pre_act).astype(jnp.bfloat16)
    down_mid = product("tgo,goq->tgq", activated, down_first).astype(jnp.bfloat16)
    down_perm = spread_blocks(down_mid)
    down_out = product("tge,geq->tgq", down_perm, down_second).reshape(count, channels)
    output = (hidden.astype(jnp.float32) + down_out).astype(jnp.bfloat16)
    grad_three = grad_out.reshape(count, local_blocks, width)
    sum_down_second = product("tge,tgq->geq", down_perm, grad_three)
    back_perm = product("tgq,geq->tge", grad_three, down_second).astype(jnp.bfloat16)
    back_mid = return_blocks(back_perm)
    sum_down_first = product("tgo,tgq->goq", activated, back_mid)
    grad_act = product("tgq,goq->tgo", back_mid, down_first)
    grad_pre = (grad_act * gelu_slope(pre_act)).astype(jnp.bfloat16)
    sum_up_second = product("tge,tgo->geo", up_perm, grad_pre)
    grad_perm = product("tgo,geo->tge", grad_pre, up_second).astype(jnp.bfloat16)
    grad_mid = return_blocks(grad_perm)
    sum_up_first = product("tkp,tkq->kpq", hidden_three, grad_mid)
    grad_inner = product("tkq,kpq->tkp", grad_mid, up_first).reshape(count, channels)
    grad_hidden = (grad_out.astype(jnp.float32) + grad_inner).astype(jnp.bfloat16)
    return (output, grad_hidden, (sum_up_first, sum_up_second, sum_down_first, sum_down_second))


def general_shards(
    activations,
    mix_first,
    twiddle,
    mix_second,
    up_first,
    up_second,
    down_first,
    down_second,
    grad_out,
):
    local_rows, local_channels = activations.shape
    block_rows = twiddle.shape[0]
    length = mix_first.shape[0]
    inputs_three = activations.reshape(block_rows, length, local_channels)
    first_pass = (product("abc,bj->ajc", inputs_three, mix_first) * twiddle[:, :, None]).astype(
        jnp.bfloat16
    )
    mixed = column_pass(first_pass, mix_second).reshape(local_rows, local_channels)
    inputs_float = activations.astype(jnp.float32)
    gating = jax.nn.sigmoid(inputs_float)
    mixed_float = mixed.astype(jnp.float32)
    hidden = (inputs_float + gating * mixed_float).astype(jnp.bfloat16)
    output, grad_hidden, grads = blocks_layer(
        hidden, grad_out, up_first, up_second, down_first, down_second
    )
    totals = lax.psum((grads[0], grads[1], grads[2], grads[3]), "seq")
    grad_float = grad_hidden.astype(jnp.float32)
    grad_mixed = (grad_float * gating).astype(jnp.bfloat16)
    back_rows = column_pass(grad_mixed.reshape(block_rows, length, local_channels), mix_second.T)
    twisted = (back_rows.astype(jnp.float32) * twiddle[:, :, None]).astype(jnp.bfloat16)
    mix_grad = product("ajc,bj->abc", twisted, mix_first).reshape(local_rows, local_channels)
    grad_inputs = (grad_float * (1.0 + gating * (1.0 - gating) * mixed_float) + mix_grad).astype(
        jnp.bfloat16
    )
    scale = 1.0 / length
    return (
        output,
        grad_inputs,
        totals[0] * scale,
        totals[1] * scale,
        totals[2] * scale,
        totals[3] * scale,
    )


def dot(left, right):
    return jnp.dot(left, right, preferred_element_type=F32)


def dot_nt(left, right):
    return lax.dot_general(left, right, (((1,), (1,)), ((), ())), preferred_element_type=F32)


def dot_tn(left, right):
    return lax.dot_general(left, right, (((0,), (0,)), ((), ())), preferred_element_type=F32)


def swap_rows(rows):
    size = rows * rows
    out = lax.broadcasted_iota(jnp.int32, (size, size), 0)
    inp = lax.broadcasted_iota(jnp.int32, (size, size), 1)
    same = (out // rows == inp % rows) & (out % rows == inp // rows)
    return jnp.where(same, 1.0, 0.0).astype(BF)


def swap_lanes(parts):
    lane = lax.broadcasted_iota(jnp.int32, parts[0].shape, 1)
    low = lane < 64
    even = (lane & 32) == 0
    x0, x1, x2, x3 = parts
    a0 = jnp.where(low, x0, pltpu.roll(x2, 64, 1))
    a2 = jnp.where(low, pltpu.roll(x0, 64, 1), x2)
    a1 = jnp.where(low, x1, pltpu.roll(x3, 64, 1))
    a3 = jnp.where(low, pltpu.roll(x1, 64, 1), x3)
    b0 = jnp.where(even, a0, pltpu.roll(a1, 32, 1))
    b1 = jnp.where(even, pltpu.roll(a0, 96, 1), a1)
    b2 = jnp.where(even, a2, pltpu.roll(a3, 32, 1))
    b3 = jnp.where(even, pltpu.roll(a2, 96, 1), a3)
    return b0, b1, b2, b3


def params(*semantics):
    return pltpu.CompilerParams(
        dimension_semantics=("arbitrary",) * len(semantics), vmem_limit_bytes=58 * 1024 * 1024
    )


def in_hbm(shape, kind=BF):
    return jax.ShapeDtypeStruct(shape, kind)


def full(shape):
    zeros = (0,) * len(shape)
    return pl.BlockSpec(shape, lambda *_: zeros)


def first_kernel(chunks, span, rows, x_ref, w_ref, tw_ref, *rest):
    outs, scratch = rest[: len(chunks)], rest[len(chunks)]
    swap = swap_rows(rows)
    low, high = chunks[0] * span, (chunks[-1] + 1) * span
    weight = w_ref[...].T[low:high, :]
    scales = tw_ref[...].T[low:high, :]
    for a in range(rows):
        value = dot(weight, x_ref[a]) * scales[:, a : a + 1]
        scratch[a] = value.astype(BF)
    size = rows * rows
    for n, out in enumerate(outs):
        _, _, height, cols = out.shape
        count = size // height
        for group in range(span // rows):
            start = n * span + group * rows
            piece = scratch[:, start : start + rows, :].reshape(size, cols)
            value = dot(swap, piece).astype(BF)
            out[group * count : (group + 1) * count, 0] = value.reshape(count, height, cols)


def first_stage(chunks, places, seq, x3, mix_first, twiddle, cols=256):
    rows, length, channels = x3.shape
    span = length // CHUNKS
    height = span * rows // seq
    return pl.pallas_call(
        functools.partial(first_kernel, chunks, span, rows),
        grid=(channels // cols,),
        in_specs=[
            pl.BlockSpec((rows, length, cols), lambda c: (0, 0, c)),
            full(mix_first.shape),
            full(twiddle.shape),
        ],
        out_specs=[
            pl.BlockSpec((seq, 1, height, cols), lambda c, part=part: (0, part, 0, c)) for part, _ in places
        ],
        out_shape=[in_hbm((seq, parts, height, channels)) for _, parts in places],
        scratch_shapes=[pltpu.VMEM((rows, span * len(chunks), cols), BF)],
        compiler_params=params(0),
        name="first",
    )(x3, mix_first, twiddle)


def second_kernel(w_ref, x_ref, *refs):
    o_ref = refs[-1]
    seq, own, rows, cols = x_ref.shape
    weight = w_ref[...]
    for j in range(own):
        value = dot(weight, x_ref[:, j].reshape(seq * rows, cols))
        o_ref[:, j] = value.astype(BF).reshape(seq, rows, cols)


def second_stage(weight, field, place, buffer, rows, cols=256):
    source, part_in = field
    part, parts = place
    seq, parts_in, height, channels = source.shape
    own = height // rows
    five = source.reshape(seq, parts_in, own, rows, channels)
    out = pl.pallas_call(
        second_kernel,
        grid=(channels // cols,),
        in_specs=[
            full(weight.shape),
            pl.BlockSpec((seq, None, own, rows, cols), lambda c: (0, part_in, 0, 0, c)),
        ]
        + ([] if buffer is None else [pl.BlockSpec(memory_space=pl.ANY)]),
        out_specs=pl.BlockSpec((seq, None, own, rows, cols), lambda c: (0, part, 0, 0, c)),
        out_shape=in_hbm((seq, parts, own, rows, channels)),
        input_output_aliases={} if buffer is None else {2: 0},
        compiler_params=params(0),
        name="second",
    )(weight, five, *(() if buffer is None else (buffer.reshape(seq, parts, own, rows, channels),)))
    return out.reshape(seq, parts, height, channels)


def spread_store(values, own_ref, send_ref):
    for half, ref in ((0, own_ref), (1, send_ref)):
        parts = [v[:, half * LANES : (half + 1) * LANES] for v in values]
        for g, part in enumerate(swap_lanes(parts)):
            ref[g] = part.astype(BF)


def gather_load(own_ref, recv_ref):
    own = swap_lanes([own_ref[g].astype(F32) for g in range(own_ref.shape[0])])
    recv = swap_lanes([recv_ref[g].astype(F32) for g in range(recv_ref.shape[0])])
    return [jnp.concatenate([a, b], axis=1).astype(BF) for a, b in zip(own, recv)]


def back_kernel(g_ref, w_ref, own_ref, send_ref):
    rows, cols, channels = g_ref.shape
    grad = g_ref[...].reshape(rows * cols, channels)
    blocks, width = w_ref.shape[0], w_ref.shape[2]
    values = [dot_nt(grad[:, h * width : (h + 1) * width], w_ref[h]) for h in range(blocks)]
    spread_store(values, own_ref, send_ref)


def back_stage(chunk, g3, down_second):
    rows, length, channels = g3.shape
    size = rows * rows
    steps = length // CHUNKS // rows
    blocks = down_second.shape[0]
    shape = jax.ShapeDtypeStruct((blocks, steps * size, LANES), BF)
    spec = pl.BlockSpec((blocks, size, LANES), lambda s: (0, s, 0))
    return pl.pallas_call(
        back_kernel,
        grid=(steps,),
        in_specs=[
            pl.BlockSpec((rows, rows, channels), lambda s: (0, chunk * steps + s, 0)),
            full(down_second.shape),
        ],
        out_specs=[spec, spec],
        out_shape=[shape, shape],
        compiler_params=params(0),
        name="back",
    )(g3, down_second)


def hidden_kernel(x_ref, m_ref, w_ref, h_ref, own_ref, send_ref):
    rows, cols, channels = x_ref.shape
    mixed = dot(swap_rows(rows), m_ref[...].reshape(rows * cols, channels))
    inputs = x_ref[...].reshape(rows * cols, channels).astype(F32)
    hidden = (inputs + jax.nn.sigmoid(inputs) * mixed).astype(BF)
    h_ref[...] = hidden
    blocks, width = w_ref.shape[0], w_ref.shape[1]
    values = [dot(hidden[:, k * width : (k + 1) * width], w_ref[k]) for k in range(blocks)]
    spread_store(values, own_ref, send_ref)


def arriving(field, size):
    source, part = field
    height, channels = source.shape[2:]
    return pl.BlockSpec((size // height, None, height, channels), lambda s: (s, part, 0, 0))


def hidden_stage(chunk, x3, mixed, up_first):
    rows, length, channels = x3.shape
    size = rows * rows
    steps = length // CHUNKS // rows
    blocks = up_first.shape[0]
    part = pl.BlockSpec((blocks, size, LANES), lambda s: (0, s, 0))
    return pl.pallas_call(
        hidden_kernel,
        grid=(steps,),
        in_specs=[
            pl.BlockSpec((rows, rows, channels), lambda s: (0, chunk * steps + s, 0)),
            arriving(mixed, size),
            full(up_first.shape),
        ],
        out_specs=[pl.BlockSpec((size, channels), lambda s: (s, 0)), part, part],
        out_shape=[
            jax.ShapeDtypeStruct((steps * size, channels), BF),
            jax.ShapeDtypeStruct((blocks, steps * size, LANES), BF),
            in_hbm((blocks, steps * size, LANES)),
        ],
        compiler_params=params(0),
        name="hidden",
    )(x3, mixed[0], up_first)


def middle_kernel(fresh, cols, *refs):
    uo, ur, bo, br, us, df = refs[:6]
    refs = refs[6:]
    if not fresh:
        sus_in, sdf_in = refs[:2]
        refs = refs[2:]
    down_own, down_send, grad_own, grad_send, sus, sdf = refs
    start = pl.program_id(1) == 0

    @pl.when(start)
    def _():
        if fresh:
            sus[...] = jnp.zeros(sus.shape, F32)
            sdf[...] = jnp.zeros(sdf.shape, F32)
        else:
            sus[...] = sus_in[...]
            sdf[...] = sdf_in[...]

    up = jnp.concatenate([uo[0], ur[0]], axis=1)
    back = jnp.concatenate([bo[0], br[0]], axis=1)
    hidden_units = us.shape[2]
    down = None
    grad = None
    for low in range(0, hidden_units, cols):
        part = slice(low, low + cols)
        z = dot(up, us[0, :, part])
        z2 = z * z
        h = 0.5 + 0.5 * jnp.tanh(z * (root_two_pi + (root_two_pi * cubic_term) * z2))
        act = (z * h).astype(BF)
        slope = h + (h - h * h) * (
            z * (2.0 * root_two_pi + (6.0 * root_two_pi * cubic_term) * z2)
        )
        pre = (dot_nt(back, df[0, part, :]) * slope).astype(BF)
        step = dot(act, df[0, part, :])
        down = step if down is None else down + step
        step = dot_nt(pre, us[0, :, part])
        grad = step if grad is None else grad + step
        sdf[0, part, :] += dot_tn(act, back)
        sus[0, :, part] += dot_tn(up, pre)
    down_own[0] = down[:, :LANES].astype(BF)
    down_send[0] = down[:, LANES:].astype(BF)
    grad_own[0] = grad[:, :LANES].astype(BF)
    grad_send[0] = grad[:, LANES:].astype(BF)


def middle_stage(up_own, up_recv, back_own, back_recv, up_second, down_first, sums, tile=512, cols=256):
    blocks, count, _ = up_own.shape
    steps = count // tile
    part = pl.BlockSpec((1, tile, LANES), lambda g, t: (g, t, 0))
    us_spec = pl.BlockSpec((1,) + up_second.shape[1:], lambda g, t: (g, 0, 0))
    df_spec = pl.BlockSpec((1,) + down_first.shape[1:], lambda g, t: (g, 0, 0))
    fresh = sums is None
    shape = jax.ShapeDtypeStruct(up_own.shape, BF)
    return pl.pallas_call(
        functools.partial(middle_kernel, fresh, cols),
        grid=(blocks, steps),
        in_specs=[part, part, part, part, us_spec, df_spec] + ([] if fresh else [us_spec, df_spec]),
        out_specs=[part] * 4 + [us_spec, df_spec],
        out_shape=[shape] * 4
        + [jax.ShapeDtypeStruct(up_second.shape, F32), jax.ShapeDtypeStruct(down_first.shape, F32)],
        input_output_aliases={} if fresh else {6: 4, 7: 5},
        compiler_params=params(0, 0),
        name="middle",
    )(up_own, up_recv, back_own, back_recv, up_second, down_first, *(() if fresh else sums))


def input_kernel(fresh, *refs):
    x_ref, g_ref, m_ref, h_ref, go, gr, w_ref = refs[:7]
    send_ref, base_ref, suf = refs[-3:]

    @pl.when(pl.program_id(0) == 0)
    def _():
        suf[...] = jnp.zeros(suf.shape, F32) if fresh else refs[7][...]

    rows, cols, channels = x_ref.shape
    size = rows * cols
    swap = swap_rows(rows)
    width = w_ref.shape[1]
    mids = gather_load(go, gr)
    x3, g3 = x_ref[...].reshape(size, channels), g_ref[...].reshape(size, channels)
    for k, mid in enumerate(mids):
        part = slice(k * width, (k + 1) * width)
        inner = dot_nt(mid, w_ref[k])
        suf[k] += dot_tn(h_ref[:, part], mid)
        grad = (g3[:, part].astype(F32) + inner).astype(BF).astype(F32)
        gating = jax.nn.sigmoid(x3[:, part].astype(F32))
        mixed = dot(swap, m_ref[:, :, part].reshape(size, width))
        send = dot(swap, (grad * gating).astype(BF)).astype(BF)
        send_ref[:, :, part] = send.reshape(send_ref.shape[0], send_ref.shape[1], width)
        base_ref[:, part] = (grad * (1.0 + gating * (1.0 - gating) * mixed)).astype(BF)


def input_stage(chunk, x3, g3, mixed, hidden, grad_own, grad_recv, up_first, sums, place, buffer):
    rows, length, channels = x3.shape
    size = rows * rows
    steps = length // CHUNKS // rows
    blocks = up_first.shape[0]
    natural = pl.BlockSpec((rows, rows, channels), lambda s: (0, chunk * steps + s, 0))
    flat = pl.BlockSpec((size, channels), lambda s: (s, 0))
    half = pl.BlockSpec((blocks, size, LANES), lambda s: (0, s, 0))
    fresh = sums is None
    wspec = full(up_first.shape)
    seq, _, height, _ = mixed[0].shape
    part, parts = place
    extra = [] if fresh else [(sums, wspec, 2)]
    if buffer is not None:
        extra.append((buffer, pl.BlockSpec(memory_space=pl.ANY), 0))
    return pl.pallas_call(
        functools.partial(input_kernel, fresh),
        grid=(steps,),
        in_specs=[natural, natural, arriving(mixed, size), flat, half, half, wspec] + [e[1] for e in extra],
        out_specs=[
            pl.BlockSpec((size // height, None, height, channels), lambda s: (s, part, 0, 0)),
            flat,
            wspec,
        ],
        out_shape=[
            in_hbm((seq, parts, height, channels)),
            jax.ShapeDtypeStruct((steps * size, channels), BF),
            jax.ShapeDtypeStruct(up_first.shape, F32),
        ],
        input_output_aliases={7 + i: e[2] for i, e in enumerate(extra)},
        compiler_params=params(0),
        name="inputs",
    )(x3, g3, mixed[0], hidden, grad_own, grad_recv, up_first, *[e[0] for e in extra])


def output_kernel(fresh, *refs):
    g_ref, h_ref, do, dr, w_ref = refs[:5]
    refs = refs[5:]
    if not fresh:
        sds_in = refs[0]
        refs = refs[2:]
    o_ref, sds = refs

    @pl.when(pl.program_id(0) == 0)
    def _():
        sds[...] = jnp.zeros(sds.shape, F32) if fresh else sds_in[...]

    rows, cols, channels = g_ref.shape
    size = rows * cols
    width = w_ref.shape[2]
    g3 = g_ref[...].reshape(size, channels)
    for h, perm in enumerate(gather_load(do, dr)):
        part = slice(h * width, (h + 1) * width)
        value = h_ref[:, part].astype(F32) + dot(perm, w_ref[h])
        o_ref[:, :, part] = value.astype(BF).reshape(rows, cols, width)
        sds[h] += dot_tn(perm, g3[:, part])


def output_stage(chunk, g3, hidden, down_own, down_recv, down_second, sums, output):
    rows, length, channels = g3.shape
    size = rows * rows
    steps = length // CHUNKS // rows
    blocks = down_second.shape[0]
    natural = pl.BlockSpec((rows, rows, channels), lambda s: (0, chunk * steps + s, 0))
    flat = pl.BlockSpec((size, channels), lambda s: (s, 0))
    part = pl.BlockSpec((blocks, size, LANES), lambda s: (0, s, 0))
    fresh = sums is None
    wspec = full(down_second.shape)
    return pl.pallas_call(
        functools.partial(output_kernel, fresh),
        grid=(steps,),
        in_specs=[natural, flat, part, part, wspec]
        + ([] if fresh else [wspec, pl.BlockSpec(memory_space=pl.ANY)]),
        out_specs=[natural, wspec],
        out_shape=[
            jax.ShapeDtypeStruct(g3.shape, BF),
            jax.ShapeDtypeStruct(down_second.shape, F32),
        ],
        input_output_aliases={} if fresh else {5: 1, 6: 0},
        compiler_params=params(0),
        name="outputs",
    )(g3, hidden, down_own, down_recv, down_second, *(() if fresh else (sums, output)))


def last_kernel(rows, w_ref, tw_ref, *refs):
    chunk_refs, base_refs = refs[:CHUNKS], refs[CHUNKS : 2 * CHUNKS]
    o_ref, scratch = refs[2 * CHUNKS :]
    size = rows * rows
    swap = swap_rows(rows)
    cols = o_ref.shape[2]
    height = chunk_refs[0].shape[1]
    count = size // height
    groups = chunk_refs[0].shape[0] // count
    for n, ref in enumerate(chunk_refs):
        for g in range(groups):
            index = n * groups + g
            piece = ref[g * count : (g + 1) * count].reshape(size, cols)
            value = dot(swap, piece) * tw_ref[:, index : index + 1]
            scratch[:, index * rows : (index + 1) * rows, :] = value.astype(BF).reshape(rows, rows, cols)
    weight = w_ref[...]
    for a in range(rows):
        base = jnp.concatenate(
            [ref[g * size + a * rows : g * size + (a + 1) * rows, :] for ref in base_refs for g in range(groups)],
            axis=0,
        )
        o_ref[a] = (dot(weight, scratch[a]) + base.astype(F32)).astype(BF)


def last_stage(rows, length, mix_first, tw_cols, fields, bases, cols=256):
    seq, _, height, channels = fields[0][0].shape
    spec = pl.BlockSpec((bases[0].shape[0], cols), lambda c: (0, c))
    field_specs = [
        pl.BlockSpec((seq, None, height, cols), lambda c, part=part: (0, part, 0, c)) for _, part in fields
    ]
    return pl.pallas_call(
        functools.partial(last_kernel, rows),
        grid=(channels // cols,),
        in_specs=[full(mix_first.shape), full(tw_cols.shape)] + field_specs + [spec] * CHUNKS,
        out_specs=pl.BlockSpec((rows, length, cols), lambda c: (0, 0, c)),
        out_shape=jax.ShapeDtypeStruct((rows, length, channels), BF),
        scratch_shapes=[pltpu.VMEM((rows, length, cols), BF)],
        compiler_params=params(0),
        name="last",
    )(mix_first, tw_cols, *[f for f, _ in fields], *bases)


def exchange(field):
    return lax.all_to_all(field, "seq", split_axis=0, concat_axis=0, tiled=True)


def partner(values):
    return lax.ppermute(values, "fsdp", [(0, 1), (1, 0)])


PLAN = (
    (((1, 0),), (("first", 1), ("back", 0), ("back", 1), ("back", 2), ("back", 3))),
    (((1, 1),), (("second", 0),)),
    (((2, 0), (1, 2)), (("second", 1),)),
    (((2, 1), (1, 3)), (("hidden", 0), ("second", 2), ("middle", 0), ("inputs", 0))),
    (((2, 2), (3, 0)), (("hidden", 1), ("second", 3), ("middle", 1), ("outputs", 0), ("inputs", 1))),
    (((2, 3), (3, 1)), (("hidden", 2), ("fourth", 0), ("middle", 2), ("outputs", 1), ("inputs", 2))),
    (((3, 2), (4, 0)), (("hidden", 3), ("fourth", 1), ("middle", 3), ("outputs", 2), ("inputs", 3))),
    (((3, 3), (4, 1)), (("fourth", 2), ("outputs", 3))),
    (((4, 2),), (("fourth", 3),)),
    (((4, 3),), ()),
)


def chunked_shards(
    seq,
    activations,
    mix_first,
    twiddle,
    mix_second,
    up_first,
    up_second,
    down_first,
    down_second,
    grad_out,
):
    local_rows, channels = activations.shape
    rows, length = twiddle.shape
    blocks, width = up_first.shape[0], up_first.shape[1]
    stride = width // NBLK
    mine = lax.axis_index("fsdp")

    def own_first(values, axis):
        return jnp.where(mine == 0, values, jnp.roll(values, LANES, axis))

    def group_rows(weight):
        shaped = weight.reshape(blocks, stride, NBLK, weight.shape[2])
        return own_first(jnp.transpose(shaped, (0, 2, 1, 3)).reshape(weight.shape), 1)

    def ungroup_rows(weight):
        shaped = own_first(weight, 1).reshape(blocks, NBLK, stride, weight.shape[2])
        return jnp.transpose(shaped, (0, 2, 1, 3)).reshape(weight.shape)

    x3 = activations.reshape(rows, length, channels)
    g3 = grad_out.reshape(rows, length, channels)
    w2, w2t = mix_second, mix_second.T
    ups_first, downs_first = own_first(up_first, 2), own_first(down_first, 2)
    ups_second, downs_second = group_rows(up_second), group_rows(down_second)
    tw_cols = jnp.transpose(twiddle.reshape(rows, length // rows, rows), (0, 2, 1)).reshape(
        rows * rows, length // rows
    )

    place = {}
    for slot, (travels, _) in enumerate(PLAN):
        for part, key in enumerate(travels):
            place[key] = (slot, part, len(travels))
    buffers, arrived, kept = {}, {}, {}
    sums, sum_first, sum_last, output = None, None, None, None

    def spot(key):
        slot, part, parts = place[key]
        return (part, parts), buffers.get(slot)

    def first(chunks):
        results = first_stage(chunks, [place[1, m][1:] for m in chunks], seq, x3, mix_first, twiddle)
        for m, sent in zip(chunks, results):
            buffers[place[1, m][0]] = sent

    def reduced(values):
        return lax.psum_scatter(
            (values * (1.0 / length)).astype(BF), "seq", scatter_dimension=0, tiled=True
        )

    def gathered(values):
        return lax.all_gather(values, "seq", axis=0, tiled=True)

    first((0,))
    for slot, (travels, tasks) in enumerate(PLAN):
        done = exchange(buffers[slot])
        for part, key in enumerate(travels):
            arrived[key] = (done, part)
        for name, n in tasks:
            if name == "first":
                first(tuple(range(1, CHUNKS)))
            elif name == "back":
                own, send = back_stage(n, g3, downs_second)
                kept["back", n] = (own, partner(send))
            elif name == "second":
                buffers[place[2, n][0]] = second_stage(w2t, arrived[1, n], *spot((2, n)), rows)
            elif name == "hidden":
                hidden, own, send = hidden_stage(n, x3, arrived[2, n], ups_first)
                kept["hidden", n] = hidden
                kept["up", n] = (own, partner(send))
            elif name == "middle":
                down_own, down_send, grad_own, grad_send, *sums = middle_stage(
                    *kept["up", n], *kept["back", n], ups_second, downs_first, sums
                )
                kept["grad", n] = (grad_own, partner(grad_send))
                kept["down", n] = (down_own, partner(down_send))
            elif name == "inputs":
                buffers[place[3, n][0]], kept["base", n], sum_first = input_stage(
                    n,
                    x3,
                    g3,
                    arrived[2, n],
                    kept["hidden", n],
                    *kept["grad", n],
                    ups_first,
                    sum_first,
                    *spot((3, n)),
                )
            elif name == "outputs":
                output, sum_last = output_stage(
                    n, g3, kept["hidden", n], *kept["down", n], downs_second, sum_last, output
                )
            else:
                buffers[place[4, n][0]] = second_stage(w2, arrived[3, n], *spot((4, n)), rows)

    parts = (
        reduced(sums[0].reshape(-1, sums[0].shape[2])),
        reduced(sums[1].reshape(-1, width)),
        reduced(jnp.concatenate([sum_first, sum_last], axis=0).reshape(-1, width)),
    )
    one, two, rest = (gathered(v) for v in parts)
    rest = rest.astype(F32).reshape(-1, width, width)
    grads = (
        own_first(rest[:blocks], 2),
        ungroup_rows(one.astype(F32).reshape(up_second.shape)),
        own_first(two.astype(F32).reshape(down_first.shape), 2),
        ungroup_rows(rest[blocks:]),
    )
    fields = [arrived[4, n] for n in range(CHUNKS)]
    bases = [kept["base", n] for n in range(CHUNKS)]
    grad_inputs = last_stage(rows, length, mix_first, tw_cols, fields, bases)
    return (
        output.reshape(local_rows, channels),
        grad_inputs.reshape(local_rows, channels),
        *grads,
    )


def shards(*args):
    _, _, twiddle, _, up_first = args[:5]
    rows, length = twiddle.shape
    blocks, width = up_first.shape[0], up_first.shape[1]
    seq = length // rows
    fits = (
        blocks * (width // NBLK) == LANES
        and 2 * blocks == NBLK
        and rows == 16
        and seq == 16
        and length % (CHUNKS * seq) == 0
    )
    if fits:
        return chunked_shards(seq, *args)
    return general_shards(*args)


def solution(mesh):
    in_specs = (
        P("seq", "fsdp"),
        P(),
        P("seq", None),
        P(),
        P("fsdp", None, None),
        P("fsdp", None, None),
        P("fsdp", None, None),
        P("fsdp", None, None),
        P("seq", "fsdp"),
    )
    out_specs = (
        P("seq", "fsdp"),
        P("seq", "fsdp"),
        P("fsdp", None, None),
        P("fsdp", None, None),
        P("fsdp", None, None),
        P("fsdp", None, None),
    )
    return jax.shard_map(shards, mesh=mesh, in_specs=in_specs, out_specs=out_specs, check_vma=False)
```

```python
import functools

import jax
import jax.numpy as jnp
from jax import lax
from jax.experimental import pallas as pl
from jax.experimental.pallas import tpu as pltpu
from jax.sharding import PartitionSpec as P


NBLK = 8
LANES = 128
CHUNKS = 4


root_two_pi = 0.7978845608028654
cubic_term = 0.044715

BF = jnp.bfloat16
F32 = jnp.float32


def gelu_value(values):
    inner = root_two_pi * (values + cubic_term * values * values * values)
    return 0.5 * values * (1.0 + jnp.tanh(inner))


def gelu_slope(values):
    inner = root_two_pi * (values + cubic_term * values * values * values)
    hyper = jnp.tanh(inner)
    return 0.5 * (1.0 + hyper) + 0.5 * values * (1.0 - hyper * hyper) * root_two_pi * (
        1.0 + 3.0 * cubic_term * values * values
    )


def product(form, left, right):
    return jnp.einsum(form, left, right, preferred_element_type=jnp.float32)


def column_pass(field, factor):
    result = product(
        "ajc,ai->ijc", lax.all_to_all(field, "seq", split_axis=1, concat_axis=0, tiled=True), factor
    ).astype(jnp.bfloat16)
    return lax.all_to_all(result, "seq", split_axis=0, concat_axis=1, tiled=True)


def shuffle_blocks(values):
    return lax.all_to_all(values, "fsdp", split_axis=2, concat_axis=1, tiled=True)


def spread_blocks(values):
    count, local_blocks, width = values.shape
    stride = width // NBLK
    received = shuffle_blocks(values)
    shaped = received.reshape(count, NBLK, local_blocks, stride)
    return jnp.transpose(shaped, (0, 2, 3, 1)).reshape(count, local_blocks, width)


def return_blocks(values):
    count, local_blocks, width = values.shape
    stride = width // NBLK
    parts = NBLK // local_blocks
    shaped = values.reshape(count, local_blocks, stride, parts, local_blocks)
    sending = jnp.transpose(shaped, (0, 1, 3, 4, 2)).reshape(count, local_blocks, width)
    received = shuffle_blocks(sending).reshape(count, NBLK, local_blocks, stride)
    return jnp.transpose(received, (0, 2, 1, 3)).reshape(count, local_blocks, width)


def blocks_layer(hidden, grad_out, up_first, up_second, down_first, down_second):
    count, channels = hidden.shape
    local_blocks, width = (up_first.shape[0], up_first.shape[1])
    hidden_three = hidden.reshape(count, local_blocks, width)
    up_mid = product("tkp,kpq->tkq", hidden_three, up_first).astype(jnp.bfloat16)
    up_perm = spread_blocks(up_mid)
    pre_act = product("tge,geo->tgo", up_perm, up_second)
    activated = gelu_value(pre_act).astype(jnp.bfloat16)
    down_mid = product("tgo,goq->tgq", activated, down_first).astype(jnp.bfloat16)
    down_perm = spread_blocks(down_mid)
    down_out = product("tge,geq->tgq", down_perm, down_second).reshape(count, channels)
    output = (hidden.astype(jnp.float32) + down_out).astype(jnp.bfloat16)
    grad_three = grad_out.reshape(count, local_blocks, width)
    sum_down_second = product("tge,tgq->geq", down_perm, grad_three)
    back_perm = product("tgq,geq->tge", grad_three, down_second).astype(jnp.bfloat16)
    back_mid = return_blocks(back_perm)
    sum_down_first = product("tgo,tgq->goq", activated, back_mid)
    grad_act = product("tgq,goq->tgo", back_mid, down_first)
    grad_pre = (grad_act * gelu_slope(pre_act)).astype(jnp.bfloat16)
    sum_up_second = product("tge,tgo->geo", up_perm, grad_pre)
    grad_perm = product("tgo,geo->tge", grad_pre, up_second).astype(jnp.bfloat16)
    grad_mid = return_blocks(grad_perm)
    sum_up_first = product("tkp,tkq->kpq", hidden_three, grad_mid)
    grad_inner = product("tkq,kpq->tkp", grad_mid, up_first).reshape(count, channels)
    grad_hidden = (grad_out.astype(jnp.float32) + grad_inner).astype(jnp.bfloat16)
    return (output, grad_hidden, (sum_up_first, sum_up_second, sum_down_first, sum_down_second))


def general_shards(
    activations,
    mix_first,
    twiddle,
    mix_second,
    up_first,
    up_second,
    down_first,
    down_second,
    grad_out,
):
    local_rows, local_channels = activations.shape
    block_rows = twiddle.shape[0]
    length = mix_first.shape[0]
    inputs_three = activations.reshape(block_rows, length, local_channels)
    first_pass = (product("abc,bj->ajc", inputs_three, mix_first) * twiddle[:, :, None]).astype(
        jnp.bfloat16
    )
    mixed = column_pass(first_pass, mix_second).reshape(local_rows, local_channels)
    inputs_float = activations.astype(jnp.float32)
    gating = jax.nn.sigmoid(inputs_float)
    mixed_float = mixed.astype(jnp.float32)
    hidden = (inputs_float + gating * mixed_float).astype(jnp.bfloat16)
    output, grad_hidden, grads = blocks_layer(
        hidden, grad_out, up_first, up_second, down_first, down_second
    )
    totals = lax.psum((grads[0], grads[1], grads[2], grads[3]), "seq")
    grad_float = grad_hidden.astype(jnp.float32)
    grad_mixed = (grad_float * gating).astype(jnp.bfloat16)
    back_rows = column_pass(grad_mixed.reshape(block_rows, length, local_channels), mix_second.T)
    twisted = (back_rows.astype(jnp.float32) * twiddle[:, :, None]).astype(jnp.bfloat16)
    mix_grad = product("ajc,bj->abc", twisted, mix_first).reshape(local_rows, local_channels)
    grad_inputs = (grad_float * (1.0 + gating * (1.0 - gating) * mixed_float) + mix_grad).astype(
        jnp.bfloat16
    )
    scale = 1.0 / length
    return (
        output,
        grad_inputs,
        totals[0] * scale,
        totals[1] * scale,
        totals[2] * scale,
        totals[3] * scale,
    )


def dot(left, right):
    return jnp.dot(left, right, preferred_element_type=F32)


def dot_nt(left, right):
    return lax.dot_general(left, right, (((1,), (1,)), ((), ())), preferred_element_type=F32)


def dot_tn(left, right):
    return lax.dot_general(left, right, (((0,), (0,)), ((), ())), preferred_element_type=F32)


def swap_rows(rows):
    size = rows * rows
    out = lax.broadcasted_iota(jnp.int32, (size, size), 0)
    inp = lax.broadcasted_iota(jnp.int32, (size, size), 1)
    same = (out // rows == inp % rows) & (out % rows == inp // rows)
    return jnp.where(same, 1.0, 0.0).astype(BF)


def swap_lanes(parts):
    lane = lax.broadcasted_iota(jnp.int32, parts[0].shape, 1)
    low = lane < 64
    even = (lane & 32) == 0
    x0, x1, x2, x3 = parts
    a0 = jnp.where(low, x0, pltpu.roll(x2, 64, 1))
    a2 = jnp.where(low, pltpu.roll(x0, 64, 1), x2)
    a1 = jnp.where(low, x1, pltpu.roll(x3, 64, 1))
    a3 = jnp.where(low, pltpu.roll(x1, 64, 1), x3)
    b0 = jnp.where(even, a0, pltpu.roll(a1, 32, 1))
    b1 = jnp.where(even, pltpu.roll(a0, 96, 1), a1)
    b2 = jnp.where(even, a2, pltpu.roll(a3, 32, 1))
    b3 = jnp.where(even, pltpu.roll(a2, 96, 1), a3)
    return b0, b1, b2, b3


def params(*semantics):
    return pltpu.CompilerParams(
        dimension_semantics=("arbitrary",) * len(semantics), vmem_limit_bytes=58 * 1024 * 1024
    )


def in_hbm(shape, kind=BF):
    return jax.ShapeDtypeStruct(shape, kind)


def full(shape):
    zeros = (0,) * len(shape)
    return pl.BlockSpec(shape, lambda *_: zeros)


def first_kernel(chunks, span, rows, x_ref, w_ref, tw_ref, *rest):
    outs, scratch = rest[: len(chunks)], rest[len(chunks)]
    swap = swap_rows(rows)
    low, high = chunks[0] * span, (chunks[-1] + 1) * span
    weight = w_ref[...].T[low:high, :]
    scales = tw_ref[...].T[low:high, :]
    for a in range(rows):
        value = dot(weight, x_ref[a]) * scales[:, a : a + 1]
        scratch[a] = value.astype(BF)
    size = rows * rows
    for n, out in enumerate(outs):
        _, _, height, cols = out.shape
        count = size // height

        @pl.loop(0, span // rows)
        def _(group, n=n, out=out):
            start = pl.multiple_of(n * span + group * rows, rows)
            piece = scratch[:, pl.ds(start, rows), :].reshape(size, cols)
            value = dot(swap, piece).astype(BF)
            out[pl.ds(group * count, count), 0] = value.reshape(count, height, cols)


def first_stage(chunks, places, seq, x3, mix_first, twiddle, cols=256):
    rows, length, channels = x3.shape
    span = length // CHUNKS
    height = span * rows // seq
    return pl.pallas_call(
        functools.partial(first_kernel, chunks, span, rows),
        grid=(channels // cols,),
        in_specs=[
            pl.BlockSpec((rows, length, cols), lambda c: (0, 0, c)),
            full(mix_first.shape),
            full(twiddle.shape),
        ],
        out_specs=[
            pl.BlockSpec((seq, 1, height, cols), lambda c, part=part: (0, part, 0, c)) for part, _ in places
        ],
        out_shape=[in_hbm((seq, parts, height, channels)) for _, parts in places],
        scratch_shapes=[pltpu.VMEM((rows, span * len(chunks), cols), BF)],
        compiler_params=params(0),
        name="first",
    )(x3, mix_first, twiddle)


def second_kernel(w_ref, x_ref, *refs):
    o_ref = refs[-1]
    seq, own, rows, cols = x_ref.shape
    weight = w_ref[...]
    for j in range(own):
        value = dot(weight, x_ref[:, j].reshape(seq * rows, cols))
        o_ref[:, j] = value.astype(BF).reshape(seq, rows, cols)


def second_stage(weight, field, place, buffer, rows, cols=256):
    source, part_in = field
    part, parts = place
    seq, parts_in, height, channels = source.shape
    own = height // rows
    five = source.reshape(seq, parts_in, own, rows, channels)
    out = pl.pallas_call(
        second_kernel,
        grid=(channels // cols,),
        in_specs=[
            full(weight.shape),
            pl.BlockSpec((seq, None, own, rows, cols), lambda c: (0, part_in, 0, 0, c)),
        ]
        + ([] if buffer is None else [pl.BlockSpec(memory_space=pl.ANY)]),
        out_specs=pl.BlockSpec((seq, None, own, rows, cols), lambda c: (0, part, 0, 0, c)),
        out_shape=in_hbm((seq, parts, own, rows, channels)),
        input_output_aliases={} if buffer is None else {2: 0},
        compiler_params=params(0),
        name="second",
    )(weight, five, *(() if buffer is None else (buffer.reshape(seq, parts, own, rows, channels),)))
    return out.reshape(seq, parts, height, channels)


def spread_store(values, own_ref, send_ref):
    for half, ref in ((0, own_ref), (1, send_ref)):
        parts = [v[:, half * LANES : (half + 1) * LANES] for v in values]
        for g, part in enumerate(swap_lanes(parts)):
            ref[g] = part.astype(BF)


def gather_load(own_ref, recv_ref):
    own = swap_lanes([own_ref[g].astype(F32) for g in range(own_ref.shape[0])])
    recv = swap_lanes([recv_ref[g].astype(F32) for g in range(recv_ref.shape[0])])
    return [jnp.concatenate([a, b], axis=1).astype(BF) for a, b in zip(own, recv)]


def offset_call(kernel, chunk, steps, in_specs, out_specs, out_shape, aliases=None, scratch=()):
    call = pl.pallas_call(
        lambda _, *refs: kernel(*refs),
        grid_spec=pltpu.PrefetchScalarGridSpec(
            num_scalar_prefetch=1,
            grid=(steps,),
            in_specs=in_specs,
            out_specs=out_specs,
            scratch_shapes=scratch,
        ),
        out_shape=out_shape,
        input_output_aliases={k + 1: v for k, v in (aliases or {}).items()},
        compiler_params=params(0),
    )
    return functools.partial(call, jnp.stack([jnp.int32(v) for v in chunk]))


def natural_block(rows, steps, channels):
    return pl.BlockSpec((rows, rows, channels), lambda s, chunk: (0, chunk[0] * steps + s, 0))


def back_kernel(g_ref, w_ref, own_ref, send_ref):
    rows, cols, channels = g_ref.shape
    grad = g_ref[...].reshape(rows * cols, channels)
    blocks, width = w_ref.shape[0], w_ref.shape[2]
    values = [dot_nt(grad[:, h * width : (h + 1) * width], w_ref[h]) for h in range(blocks)]
    spread_store(values, own_ref, send_ref)


def back_stage(g3, down_second):
    rows, length, channels = g3.shape
    size = rows * rows
    blocks = down_second.shape[0]
    shape = jax.ShapeDtypeStruct((blocks, rows * length, LANES), BF)
    spec = pl.BlockSpec((blocks, size, LANES), lambda s: (0, s, 0))
    return pl.pallas_call(
        back_kernel,
        grid=(length // rows,),
        in_specs=[pl.BlockSpec((rows, rows, channels), lambda s: (0, s, 0)), full(down_second.shape)],
        out_specs=[spec, spec],
        out_shape=[shape, shape],
        compiler_params=params(0),
        name="back",
    )(g3, down_second)


def hidden_kernel(x_ref, m_ref, w_ref, h_ref, own_ref, send_ref, mids):
    rows, cols, _ = x_ref.shape
    size = rows * cols
    blocks, width = w_ref.shape[0], w_ref.shape[1]
    swap = swap_rows(rows)

    @pl.loop(0, blocks)
    def _(k):
        part = pl.ds(pl.multiple_of(k * width, width), width)
        mixed = dot(swap, m_ref[:, :, part].reshape(size, width))
        inputs = x_ref[:, :, part].reshape(size, width).astype(F32)
        hidden = (inputs + jax.nn.sigmoid(inputs) * mixed).astype(BF)
        h_ref[:, part] = hidden
        mids[k] = dot(hidden, w_ref[k])

    spread_store([mids[k] for k in range(blocks)], own_ref, send_ref)


def arriving(field, size):
    source, part = field
    height, channels = source.shape[2:]
    return pl.BlockSpec((size // height, None, height, channels), lambda s, *_: (s, part, 0, 0))


def hidden_stage(chunk, x3, mixed, up_first):
    rows, length, channels = x3.shape
    size = rows * rows
    steps = length // CHUNKS // rows
    blocks = up_first.shape[0]
    part = pl.BlockSpec((blocks, size, LANES), lambda s, _: (0, s, 0))
    return offset_call(
        hidden_kernel,
        (chunk,),
        steps,
        [natural_block(rows, steps, channels), arriving(mixed, size), full(up_first.shape)],
        [pl.BlockSpec((size, channels), lambda s, _: (s, 0)), part, part],
        [
            jax.ShapeDtypeStruct((steps * size, channels), BF),
            jax.ShapeDtypeStruct((blocks, steps * size, LANES), BF),
            in_hbm((blocks, steps * size, LANES)),
        ],
        scratch=[pltpu.VMEM((blocks, size, 2 * LANES), F32)],
    )(x3, mixed[0], up_first)


def middle_kernel(cols, *refs):
    uo, ur, bo, br, us, df, sus_in, sdf_in = refs[:8]
    down_own, down_send, grad_own, grad_send, sus, sdf, down_sum, grad_sum = refs[8:]
    start = pl.program_id(1) == 0

    @pl.when(start)
    def _():
        sus[...] = sus_in[...]
        sdf[...] = sdf_in[...]

    up = jnp.concatenate([uo[0], ur[0]], axis=1)
    back = jnp.concatenate([bo[0], br[0]], axis=1)
    hidden_units = us.shape[2]
    down_sum[...] = jnp.zeros(down_sum.shape, F32)
    grad_sum[...] = jnp.zeros(grad_sum.shape, F32)

    @pl.loop(0, hidden_units // (2 * cols))
    def _(pair):
        down, grad = None, None
        for side in range(2):
            part = pl.ds(pl.multiple_of((2 * pair + side) * cols, cols), cols)
            z = dot(up, us[0, :, part])
            z2 = z * z
            h = 0.5 + 0.5 * jnp.tanh(z * (root_two_pi + (root_two_pi * cubic_term) * z2))
            act = (z * h).astype(BF)
            slope = h + (h - h * h) * (
                z * (2.0 * root_two_pi + (6.0 * root_two_pi * cubic_term) * z2)
            )
            pre = (dot_nt(back, df[0, part, :]) * slope).astype(BF)
            step = dot(act, df[0, part, :])
            down = step if down is None else down + step
            step = dot_nt(pre, us[0, :, part])
            grad = step if grad is None else grad + step
            sdf[0, part, :] += dot_tn(act, back)
            sus[0, :, part] += dot_tn(up, pre)
        down_sum[...] += down
        grad_sum[...] += grad

    down, grad = down_sum[...], grad_sum[...]
    down_own[0] = down[:, :LANES].astype(BF)
    down_send[0] = down[:, LANES:].astype(BF)
    grad_own[0] = grad[:, :LANES].astype(BF)
    grad_send[0] = grad[:, LANES:].astype(BF)


def middle_stage(chunk, up_own, up_recv, back_own, back_recv, up_second, down_first, sums, tile=512, cols=256):
    blocks, count, _ = up_own.shape
    steps = count // tile
    part = pl.BlockSpec((1, tile, LANES), lambda g, t: (g, t, 0))
    shifted = pl.BlockSpec((1, tile, LANES), lambda g, t: (g, chunk * steps + t, 0))
    us_spec = pl.BlockSpec((1,) + up_second.shape[1:], lambda g, t: (g, 0, 0))
    df_spec = pl.BlockSpec((1,) + down_first.shape[1:], lambda g, t: (g, 0, 0))
    shape = jax.ShapeDtypeStruct(up_own.shape, BF)
    return pl.pallas_call(
        functools.partial(middle_kernel, cols),
        grid=(blocks, steps),
        in_specs=[part, part, shifted, shifted, us_spec, df_spec, us_spec, df_spec],
        out_specs=[part] * 4 + [us_spec, df_spec],
        out_shape=[shape] * 4
        + [jax.ShapeDtypeStruct(up_second.shape, F32), jax.ShapeDtypeStruct(down_first.shape, F32)],
        scratch_shapes=[pltpu.VMEM((tile, 2 * LANES), F32)] * 2,
        input_output_aliases={6: 4, 7: 5},
        compiler_params=params(0, 0),
        name="middle",
    )(up_own, up_recv, back_own, back_recv, up_second, down_first, *sums)


def input_kernel(*refs):
    x_ref, g_ref, m_ref, h_ref, go, gr, w_ref, suf_in = refs[:8]
    send_ref, base_ref, suf, mids = refs[-4:]

    @pl.when(pl.program_id(0) == 0)
    def _():
        suf[...] = suf_in[...]

    rows, cols, _ = x_ref.shape
    size = rows * cols
    swap = swap_rows(rows)
    width = w_ref.shape[1]
    for k, mid in enumerate(gather_load(go, gr)):
        mids[k] = mid

    @pl.loop(0, w_ref.shape[0])
    def _(k):
        part = pl.ds(pl.multiple_of(k * width, width), width)
        mid = mids[k]
        inner = dot_nt(mid, w_ref[k])
        suf[k] += dot_tn(h_ref[:, part], mid)
        grad = g_ref[:, :, part].reshape(size, width).astype(F32) + inner
        grad = grad.astype(BF).astype(F32)
        gating = jax.nn.sigmoid(x_ref[:, :, part].reshape(size, width).astype(F32))
        mixed = dot(swap, m_ref[:, :, part].reshape(size, width))
        send = dot(swap, (grad * gating).astype(BF)).astype(BF)
        send_ref[:, :, part] = send.reshape(send_ref.shape[0], send_ref.shape[1], width)
        base_ref[:, part] = (grad * (1.0 + gating * (1.0 - gating) * mixed)).astype(BF)


def input_stage(chunk, x3, g3, mixed, hidden, grad_own, grad_recv, up_first, sums, place, buffer):
    rows, length, channels = x3.shape
    size = rows * rows
    steps = length // CHUNKS // rows
    blocks = up_first.shape[0]
    flat = pl.BlockSpec((size, channels), lambda s, _: (s, 0))
    half = pl.BlockSpec((blocks, size, LANES), lambda s, _: (0, s, 0))
    natural = natural_block(rows, steps, channels)
    wspec = full(up_first.shape)
    seq, _, height, _ = mixed[0].shape
    part, parts = place
    return offset_call(
        input_kernel,
        (chunk, part),
        steps,
        [natural, natural, arriving(mixed, size), flat, half, half, wspec, wspec, pl.BlockSpec(memory_space=pl.ANY)],
        [
            pl.BlockSpec((size // height, None, height, channels), lambda s, at: (s, at[1], 0, 0)),
            flat,
            wspec,
        ],
        [
            in_hbm((seq, parts, height, channels)),
            jax.ShapeDtypeStruct((steps * size, channels), BF),
            jax.ShapeDtypeStruct(up_first.shape, F32),
        ],
        {7: 2, 8: 0},
        [pltpu.VMEM((blocks, size, 2 * LANES), BF)],
    )(x3, g3, mixed[0], hidden, grad_own, grad_recv, up_first, sums, buffer)


def output_kernel(fresh, *refs):
    g_ref, h_ref, do, dr, w_ref = refs[:5]
    refs = refs[5:]
    if not fresh:
        sds_in = refs[0]
        refs = refs[2:]
    o_ref, sds, perms = refs

    @pl.when(pl.program_id(0) == 0)
    def _():
        sds[...] = jnp.zeros(sds.shape, F32) if fresh else sds_in[...]

    rows, cols, _ = g_ref.shape
    size = rows * cols
    width = w_ref.shape[2]
    for h, perm in enumerate(gather_load(do, dr)):
        perms[h] = perm

    @pl.loop(0, w_ref.shape[0])
    def _(h):
        part = pl.ds(pl.multiple_of(h * width, width), width)
        perm = perms[h]
        value = h_ref[:, part].astype(F32) + dot(perm, w_ref[h])
        o_ref[:, :, part] = value.astype(BF).reshape(rows, cols, width)
        sds[h] += dot_tn(perm, g_ref[:, :, part].reshape(size, width))


def output_stage(chunk, g3, hidden, down_own, down_recv, down_second, sums, output):
    rows, length, channels = g3.shape
    size = rows * rows
    steps = length // CHUNKS // rows
    blocks = down_second.shape[0]
    flat = pl.BlockSpec((size, channels), lambda s, _: (s, 0))
    part = pl.BlockSpec((blocks, size, LANES), lambda s, _: (0, s, 0))
    natural = natural_block(rows, steps, channels)
    fresh = sums is None
    wspec = full(down_second.shape)
    return offset_call(
        functools.partial(output_kernel, fresh),
        (chunk,),
        steps,
        [natural, flat, part, part, wspec] + ([] if fresh else [wspec, pl.BlockSpec(memory_space=pl.ANY)]),
        [natural, wspec],
        [jax.ShapeDtypeStruct(g3.shape, BF), jax.ShapeDtypeStruct(down_second.shape, F32)],
        {} if fresh else {5: 1, 6: 0},
        [pltpu.VMEM((blocks, size, 2 * LANES), BF)],
    )(g3, hidden, down_own, down_recv, down_second, *(() if fresh else (sums, output)))


def last_kernel(rows, w_ref, tw_ref, *refs):
    chunk_refs, base_refs = refs[:CHUNKS], refs[CHUNKS : 2 * CHUNKS]
    o_ref, scratch = refs[2 * CHUNKS :]
    size = rows * rows
    swap = swap_rows(rows)
    cols = o_ref.shape[2]
    height = chunk_refs[0].shape[1]
    count = size // height
    groups = chunk_refs[0].shape[0] // count
    for n, ref in enumerate(chunk_refs):
        for g in range(groups):
            index = n * groups + g
            piece = ref[g * count : (g + 1) * count].reshape(size, cols)
            value = dot(swap, piece) * tw_ref[:, index : index + 1]
            scratch[:, index * rows : (index + 1) * rows, :] = value.astype(BF).reshape(rows, rows, cols)
    weight = w_ref[...]
    for a in range(rows):
        base = jnp.concatenate(
            [ref[g * size + a * rows : g * size + (a + 1) * rows, :] for ref in base_refs for g in range(groups)],
            axis=0,
        )
        o_ref[a] = (dot(weight, scratch[a]) + base.astype(F32)).astype(BF)


def last_stage(rows, length, mix_first, tw_cols, fields, bases, cols=256):
    seq, _, height, channels = fields[0][0].shape
    spec = pl.BlockSpec((bases[0].shape[0], cols), lambda c: (0, c))
    field_specs = [
        pl.BlockSpec((seq, None, height, cols), lambda c, part=part: (0, part, 0, c)) for _, part in fields
    ]
    return pl.pallas_call(
        functools.partial(last_kernel, rows),
        grid=(channels // cols,),
        in_specs=[full(mix_first.shape), full(tw_cols.shape)] + field_specs + [spec] * CHUNKS,
        out_specs=pl.BlockSpec((rows, length, cols), lambda c: (0, 0, c)),
        out_shape=jax.ShapeDtypeStruct((rows, length, channels), BF),
        scratch_shapes=[pltpu.VMEM((rows, length, cols), BF)],
        compiler_params=params(0),
        name="last",
    )(mix_first, tw_cols, *[f for f, _ in fields], *bases)


def group_matrix(mine, width, blocks):
    stride = width // NBLK
    out = lax.broadcasted_iota(jnp.int32, (width, width), 0)
    inp = lax.broadcasted_iota(jnp.int32, (width, width), 1)
    k = inp % NBLK
    half = k // blocks
    half = half + mine - 2 * half * mine
    target = half * LANES + (k % blocks) * stride + inp // NBLK
    return jnp.where(out == target, 1.0, 0.0).astype(BF)


def copy_halves(mine, source, targets):
    for own in range(2):

        @pl.when(mine == own)
        def _():
            for get, put, kind in zip(source, targets, [t[0].dtype for t in targets]):
                value = get()
                low, high = value[..., :LANES], value[..., LANES:]
                ref, index = put
                ref[(*index, slice(0, LANES))] = (high if own else low).astype(kind)
                ref[(*index, slice(LANES, 2 * LANES))] = (low if own else high).astype(kind)


def prepare_kernel(mine_ref, uf, us, df, ds, uf_out, us_out, df_out, ds_out, *sums):
    for ref in sums:
        ref[...] = jnp.zeros(ref.shape, F32)
    mine = mine_ref[0]
    matrix = group_matrix(mine, ds.shape[1], NBLK // 2)
    copy_halves(mine, (lambda: uf[0], lambda: df[0]), ((uf_out, (0, slice(None))), (df_out, (0, slice(None)))))
    us_out[0] = dot(matrix, us[0]).astype(BF)
    ds_out[0] = dot(matrix, ds[0]).astype(BF)


def by_block(array):
    return pl.BlockSpec((1,) + array.shape[1:], lambda g, *_: (g, 0, 0))


def prepare_stage(mine, weights):
    specs = [by_block(w) for w in weights]
    return pl.pallas_call(
        prepare_kernel,
        grid_spec=pltpu.PrefetchScalarGridSpec(
            num_scalar_prefetch=1,
            grid=(weights[0].shape[0],),
            in_specs=specs,
            out_specs=specs + specs[:3],
        ),
        out_shape=[jax.ShapeDtypeStruct(w.shape, BF) for w in weights]
        + [jax.ShapeDtypeStruct(w.shape, F32) for w in weights[:3]],
        compiler_params=params(0),
        name="prepare",
    )(mine, *weights)


def collect_kernel(scale, sus, sdf, suf, sds, out):
    width = suf.shape[1]
    row = 0
    pieces = [sus[0, :, low : low + width] for low in range(0, sus.shape[2], width)]
    pieces += [sdf[0], suf[0], sds[0]]
    for piece in pieces:
        out[0, row : row + piece.shape[0], :] = (piece * scale).astype(BF)
        row += piece.shape[0]


def collect_stage(scale, sums):
    blocks, width = sums[2].shape[:2]
    height = sum(v.shape[1] * v.shape[2] for v in sums) // width
    return pl.pallas_call(
        functools.partial(collect_kernel, scale),
        grid=(blocks,),
        in_specs=[by_block(v) for v in sums],
        out_specs=pl.BlockSpec((1, height, width), lambda g: (g, 0, 0)),
        out_shape=jax.ShapeDtypeStruct((blocks, height, width), BF),
        compiler_params=params(0),
        name="collect",
    )(*sums)


def finish_kernel(mine_ref, whole, uf, us, df, ds):
    mine = mine_ref[0]
    width = ds.shape[1]
    matrix = group_matrix(mine, width, NBLK // 2)
    row = us.shape[2] // width * width

    @pl.loop(0, us.shape[2] // width)
    def _(n):
        here = pl.ds(pl.multiple_of(n * width, width), width)
        us[0, :, here] = dot_tn(matrix, whole[0, here, :])

    tall = df.shape[1]
    down, up = whole.at[0, row : row + tall, :], whole.at[0, row + tall : row + tall + width, :]
    copy_halves(
        mine,
        (lambda: down[...], lambda: up[...]),
        ((df, (0, slice(None))), (uf, (0, slice(None)))),
    )
    row += tall + width
    ds[0] = dot_tn(matrix, whole[0, row : row + width, :])


def finish_stage(mine, whole, weights):
    specs = [by_block(w) for w in weights]
    return pl.pallas_call(
        finish_kernel,
        grid_spec=pltpu.PrefetchScalarGridSpec(
            num_scalar_prefetch=1, grid=(whole.shape[0],), in_specs=[by_block(whole)], out_specs=specs
        ),
        out_shape=[jax.ShapeDtypeStruct(w.shape, F32) for w in weights],
        compiler_params=params(0),
        name="finish",
    )(mine, whole)


def exchange(field):
    return lax.all_to_all(field, "seq", split_axis=0, concat_axis=0, tiled=True)


def partner(values):
    return lax.ppermute(values, "fsdp", [(0, 1), (1, 0)])


PLAN = (
    (((1, 0),), (("first", 1), ("prepare", 0), ("back", 0))),
    (((1, 1),), (("second", 0),)),
    (((2, 0), (1, 2)), (("second", 1),)),
    (((2, 1), (1, 3)), (("hidden", 0), ("second", 2), ("middle", 0), ("inputs", 0))),
    (((2, 2), (3, 0)), (("hidden", 1), ("second", 3), ("middle", 1), ("outputs", 0), ("inputs", 1))),
    (((2, 3), (3, 1)), (("hidden", 2), ("fourth", 0), ("middle", 2), ("outputs", 1), ("inputs", 2))),
    (((3, 2), (4, 0)), (("hidden", 3), ("fourth", 1), ("middle", 3), ("outputs", 2), ("inputs", 3))),
    (((3, 3), (4, 1)), (("fourth", 2), ("outputs", 3), ("collect", 0))),
    (((4, 2),), (("fourth", 3),)),
    (((4, 3),), (("finish", 0),)),
)


def tie(value, others):
    return lax.optimization_barrier((value, others))[0]


def chunked_shards(
    seq,
    activations,
    mix_first,
    twiddle,
    mix_second,
    up_first,
    up_second,
    down_first,
    down_second,
    grad_out,
):
    local_rows, channels = activations.shape
    rows, length = twiddle.shape
    mine = lax.axis_index("fsdp").astype(jnp.int32).reshape(1)
    weights = (up_first, up_second, down_first, down_second)

    x3 = activations.reshape(rows, length, channels)
    g3 = grad_out.reshape(rows, length, channels)
    w2, w2t = mix_second, mix_second.T
    tw_cols = jnp.transpose(twiddle.reshape(rows, length // rows, rows), (0, 2, 1)).reshape(
        rows * rows, length // rows
    )

    place = {}
    for slot, (travels, _) in enumerate(PLAN):
        for part, key in enumerate(travels):
            place[key] = (slot, part, len(travels))
    buffers, arrived, kept = {}, {}, {}
    halves = [list(range(seq // 2)), list(range(seq // 2, seq))]
    sum_last, output = None, None

    def spot(key):
        slot, part, parts = place[key]
        return (part, parts), buffers.get(slot)

    def first(chunks):
        results = first_stage(chunks, [place[1, m][1:] for m in chunks], seq, x3, mix_first, twiddle)
        for m, sent in zip(chunks, results):
            buffers[place[1, m][0]] = sent

    first((0,))
    ups_first, ups_second, downs_first, downs_second, sum_first, *sums = prepare_stage(mine, weights)
    for slot, (travels, tasks) in enumerate(PLAN):
        done = exchange(buffers[slot])
        for part, key in enumerate(travels):
            arrived[key] = (done, part)
        for name, n in tasks:
            if name == "first":
                first(tuple(range(1, CHUNKS)))
            elif name == "back":
                own, send = back_stage(g3, downs_second)
                back = (own, partner(send))
            elif name == "second":
                buffers[place[2, n][0]] = second_stage(w2t, arrived[1, n], *spot((2, n)), rows)
            elif name == "hidden":
                hidden, own, send = hidden_stage(n, x3, arrived[2, n], ups_first)
                kept["hidden", n] = hidden
                kept["up", n] = (own, partner(send))
            elif name == "middle":
                down_own, down_send, grad_own, grad_send, *sums = middle_stage(
                    n, *kept["up", n], *back, ups_second, downs_first, sums
                )
                kept["grad", n] = (grad_own, partner(grad_send))
                kept["down", n] = (down_own, partner(down_send))
            elif name == "inputs":
                buffers[place[3, n][0]], kept["base", n], sum_first = input_stage(
                    n,
                    x3,
                    g3,
                    arrived[2, n],
                    kept["hidden", n],
                    *kept["grad", n],
                    ups_first,
                    sum_first,
                    *spot((3, n)),
                )
            elif name == "outputs":
                output, sum_last = output_stage(
                    n, g3, kept["hidden", n], *kept["down", n], downs_second, sum_last, output
                )
            elif name == "fourth":
                buffers[place[4, n][0]] = second_stage(w2, arrived[3, n], *spot((4, n)), rows)

    collected = collect_stage(1.0 / length, (*sums, sum_first, sum_last))
    part = lax.psum_scatter(
        collected.reshape(-1, collected.shape[2]),
        "seq",
        scatter_dimension=0,
        axis_index_groups=halves,
        tiled=True,
    )
    other = lax.ppermute(part, "seq", [(d, (d + seq // 2) % seq) for d in range(seq)])
    other = tie(other, buffers[place[4, CHUNKS - 1][0]])
    part = (part.astype(F32) + other.astype(F32)).astype(BF)
    whole = lax.all_gather(part, "seq", axis=0, axis_index_groups=halves, tiled=True)
    grads = finish_stage(mine, whole.reshape(collected.shape), weights)
    tw_cols = tie(tw_cols, grads)
    fields = [arrived[4, n] for n in range(CHUNKS)]
    bases = [kept["base", n] for n in range(CHUNKS)]
    grad_inputs = last_stage(rows, length, mix_first, tw_cols, fields, bases)
    return (
        output.reshape(local_rows, channels),
        grad_inputs.reshape(local_rows, channels),
        *grads,
    )


def shards(*args):
    _, _, twiddle, _, up_first = args[:5]
    rows, length = twiddle.shape
    blocks, width = up_first.shape[0], up_first.shape[1]
    seq = length // rows
    fits = (
        blocks * (width // NBLK) == LANES
        and 2 * blocks == NBLK
        and rows == 16
        and seq == 16
        and length % (CHUNKS * seq) == 0
    )
    if fits:
        return chunked_shards(seq, *args)
    return general_shards(*args)


def solution(mesh):
    in_specs = (
        P("seq", "fsdp"),
        P(),
        P("seq", None),
        P(),
        P("fsdp", None, None),
        P("fsdp", None, None),
        P("fsdp", None, None),
        P("fsdp", None, None),
        P("seq", "fsdp"),
    )
    out_specs = (
        P("seq", "fsdp"),
        P("seq", "fsdp"),
        P("fsdp", None, None),
        P("fsdp", None, None),
        P("fsdp", None, None),
        P("fsdp", None, None),
    )
    return jax.shard_map(shards, mesh=mesh, in_specs=in_specs, out_specs=out_specs, check_vma=False)
```

```python
import functools

import jax
import jax.numpy as jnp
from jax import lax
from jax.experimental import pallas as pl
from jax.experimental.pallas import tpu as pltpu
from jax.sharding import PartitionSpec as P


NBLK = 8
LANES = 128
CHUNKS = 4


root_two_pi = 0.7978845608028654
cubic_term = 0.044715

BF = jnp.bfloat16
F32 = jnp.float32


def gelu_value(values):
    inner = root_two_pi * (values + cubic_term * values * values * values)
    return 0.5 * values * (1.0 + jnp.tanh(inner))


def gelu_slope(values):
    inner = root_two_pi * (values + cubic_term * values * values * values)
    hyper = jnp.tanh(inner)
    return 0.5 * (1.0 + hyper) + 0.5 * values * (1.0 - hyper * hyper) * root_two_pi * (
        1.0 + 3.0 * cubic_term * values * values
    )


def product(form, left, right):
    return jnp.einsum(form, left, right, preferred_element_type=jnp.float32)


def column_pass(field, factor):
    result = product(
        "ajc,ai->ijc", lax.all_to_all(field, "seq", split_axis=1, concat_axis=0, tiled=True), factor
    ).astype(jnp.bfloat16)
    return lax.all_to_all(result, "seq", split_axis=0, concat_axis=1, tiled=True)


def shuffle_blocks(values):
    return lax.all_to_all(values, "fsdp", split_axis=2, concat_axis=1, tiled=True)


def spread_blocks(values):
    count, local_blocks, width = values.shape
    stride = width // NBLK
    received = shuffle_blocks(values)
    shaped = received.reshape(count, NBLK, local_blocks, stride)
    return jnp.transpose(shaped, (0, 2, 3, 1)).reshape(count, local_blocks, width)


def return_blocks(values):
    count, local_blocks, width = values.shape
    stride = width // NBLK
    parts = NBLK // local_blocks
    shaped = values.reshape(count, local_blocks, stride, parts, local_blocks)
    sending = jnp.transpose(shaped, (0, 1, 3, 4, 2)).reshape(count, local_blocks, width)
    received = shuffle_blocks(sending).reshape(count, NBLK, local_blocks, stride)
    return jnp.transpose(received, (0, 2, 1, 3)).reshape(count, local_blocks, width)


def blocks_layer(hidden, grad_out, up_first, up_second, down_first, down_second):
    count, channels = hidden.shape
    local_blocks, width = (up_first.shape[0], up_first.shape[1])
    hidden_three = hidden.reshape(count, local_blocks, width)
    up_mid = product("tkp,kpq->tkq", hidden_three, up_first).astype(jnp.bfloat16)
    up_perm = spread_blocks(up_mid)
    pre_act = product("tge,geo->tgo", up_perm, up_second)
    activated = gelu_value(pre_act).astype(jnp.bfloat16)
    down_mid = product("tgo,goq->tgq", activated, down_first).astype(jnp.bfloat16)
    down_perm = spread_blocks(down_mid)
    down_out = product("tge,geq->tgq", down_perm, down_second).reshape(count, channels)
    output = (hidden.astype(jnp.float32) + down_out).astype(jnp.bfloat16)
    grad_three = grad_out.reshape(count, local_blocks, width)
    sum_down_second = product("tge,tgq->geq", down_perm, grad_three)
    back_perm = product("tgq,geq->tge", grad_three, down_second).astype(jnp.bfloat16)
    back_mid = return_blocks(back_perm)
    sum_down_first = product("tgo,tgq->goq", activated, back_mid)
    grad_act = product("tgq,goq->tgo", back_mid, down_first)
    grad_pre = (grad_act * gelu_slope(pre_act)).astype(jnp.bfloat16)
    sum_up_second = product("tge,tgo->geo", up_perm, grad_pre)
    grad_perm = product("tgo,geo->tge", grad_pre, up_second).astype(jnp.bfloat16)
    grad_mid = return_blocks(grad_perm)
    sum_up_first = product("tkp,tkq->kpq", hidden_three, grad_mid)
    grad_inner = product("tkq,kpq->tkp", grad_mid, up_first).reshape(count, channels)
    grad_hidden = (grad_out.astype(jnp.float32) + grad_inner).astype(jnp.bfloat16)
    return (output, grad_hidden, (sum_up_first, sum_up_second, sum_down_first, sum_down_second))


def general_shards(
    activations,
    mix_first,
    twiddle,
    mix_second,
    up_first,
    up_second,
    down_first,
    down_second,
    grad_out,
):
    local_rows, local_channels = activations.shape
    block_rows = twiddle.shape[0]
    length = mix_first.shape[0]
    inputs_three = activations.reshape(block_rows, length, local_channels)
    first_pass = (product("abc,bj->ajc", inputs_three, mix_first) * twiddle[:, :, None]).astype(
        jnp.bfloat16
    )
    mixed = column_pass(first_pass, mix_second).reshape(local_rows, local_channels)
    inputs_float = activations.astype(jnp.float32)
    gating = jax.nn.sigmoid(inputs_float)
    mixed_float = mixed.astype(jnp.float32)
    hidden = (inputs_float + gating * mixed_float).astype(jnp.bfloat16)
    output, grad_hidden, grads = blocks_layer(
        hidden, grad_out, up_first, up_second, down_first, down_second
    )
    totals = lax.psum((grads[0], grads[1], grads[2], grads[3]), "seq")
    grad_float = grad_hidden.astype(jnp.float32)
    grad_mixed = (grad_float * gating).astype(jnp.bfloat16)
    back_rows = column_pass(grad_mixed.reshape(block_rows, length, local_channels), mix_second.T)
    twisted = (back_rows.astype(jnp.float32) * twiddle[:, :, None]).astype(jnp.bfloat16)
    mix_grad = product("ajc,bj->abc", twisted, mix_first).reshape(local_rows, local_channels)
    grad_inputs = (grad_float * (1.0 + gating * (1.0 - gating) * mixed_float) + mix_grad).astype(
        jnp.bfloat16
    )
    scale = 1.0 / length
    return (
        output,
        grad_inputs,
        totals[0] * scale,
        totals[1] * scale,
        totals[2] * scale,
        totals[3] * scale,
    )


def dot(left, right):
    return jnp.dot(left, right, preferred_element_type=F32)


def dot_nt(left, right):
    return lax.dot_general(left, right, (((1,), (1,)), ((), ())), preferred_element_type=F32)


def dot_tn(left, right):
    return lax.dot_general(left, right, (((0,), (0,)), ((), ())), preferred_element_type=F32)


def swap_rows(rows):
    size = rows * rows
    out = lax.broadcasted_iota(jnp.int32, (size, size), 0)
    inp = lax.broadcasted_iota(jnp.int32, (size, size), 1)
    same = (out // rows == inp % rows) & (out % rows == inp // rows)
    return jnp.where(same, 1.0, 0.0).astype(BF)


def swap_lanes(parts):
    lane = lax.broadcasted_iota(jnp.int32, parts[0].shape, 1)
    low = lane < 64
    even = (lane & 32) == 0
    x0, x1, x2, x3 = parts
    a0 = jnp.where(low, x0, pltpu.roll(x2, 64, 1))
    a2 = jnp.where(low, pltpu.roll(x0, 64, 1), x2)
    a1 = jnp.where(low, x1, pltpu.roll(x3, 64, 1))
    a3 = jnp.where(low, pltpu.roll(x1, 64, 1), x3)
    b0 = jnp.where(even, a0, pltpu.roll(a1, 32, 1))
    b1 = jnp.where(even, pltpu.roll(a0, 96, 1), a1)
    b2 = jnp.where(even, a2, pltpu.roll(a3, 32, 1))
    b3 = jnp.where(even, pltpu.roll(a2, 96, 1), a3)
    return b0, b1, b2, b3


def params(*semantics):
    return pltpu.CompilerParams(
        dimension_semantics=("arbitrary",) * len(semantics), vmem_limit_bytes=58 * 1024 * 1024
    )


def in_hbm(shape, kind=BF):
    return jax.ShapeDtypeStruct(shape, kind)


def full(shape):
    zeros = (0,) * len(shape)
    return pl.BlockSpec(shape, lambda *_: zeros)


def first_kernel(chunks, span, rows, x_ref, w_ref, tw_ref, *rest):
    outs, scratch = rest[: len(chunks)], rest[len(chunks)]
    swap = swap_rows(rows)
    low, high = chunks[0] * span, (chunks[-1] + 1) * span
    weight = w_ref[...].T[low:high, :]
    scales = tw_ref[...].T[low:high, :]
    for a in range(rows):
        value = dot(weight, x_ref[a]) * scales[:, a : a + 1]
        scratch[a] = value.astype(BF)
    size = rows * rows
    for n, out in enumerate(outs):
        _, _, height, cols = out.shape
        count = size // height
        for group in range(span // rows):
            start = n * span + group * rows
            piece = scratch[:, start : start + rows, :].reshape(size, cols)
            value = dot(swap, piece).astype(BF)
            out[group * count : (group + 1) * count, 0] = value.reshape(count, height, cols)


def first_stage(chunks, places, seq, x3, mix_first, twiddle, cols=256):
    rows, length, channels = x3.shape
    span = length // CHUNKS
    height = span * rows // seq
    return pl.pallas_call(
        functools.partial(first_kernel, chunks, span, rows),
        grid=(channels // cols,),
        in_specs=[
            pl.BlockSpec((rows, length, cols), lambda c: (0, 0, c)),
            full(mix_first.shape),
            full(twiddle.shape),
        ],
        out_specs=[
            pl.BlockSpec((seq, 1, height, cols), lambda c, part=part: (0, part, 0, c)) for part, _ in places
        ],
        out_shape=[in_hbm((seq, parts, height, channels)) for _, parts in places],
        scratch_shapes=[pltpu.VMEM((rows, span * len(chunks), cols), BF)],
        compiler_params=params(0),
        name="first",
    )(x3, mix_first, twiddle)


def second_kernel(w_ref, x_ref, *refs):
    o_ref = refs[-1]
    seq, own, rows, cols = x_ref.shape
    weight = w_ref[...]
    for j in range(own):
        value = dot(weight, x_ref[:, j].reshape(seq * rows, cols))
        o_ref[:, j] = value.astype(BF).reshape(seq, rows, cols)


def second_stage(weight, field, place, buffer, rows, cols=256):
    source, part_in = field
    part, parts = place
    seq, parts_in, height, channels = source.shape
    own = height // rows
    five = source.reshape(seq, parts_in, own, rows, channels)
    out = pl.pallas_call(
        second_kernel,
        grid=(channels // cols,),
        in_specs=[
            full(weight.shape),
            pl.BlockSpec((seq, None, own, rows, cols), lambda c: (0, part_in, 0, 0, c)),
        ]
        + ([] if buffer is None else [pl.BlockSpec(memory_space=pl.ANY)]),
        out_specs=pl.BlockSpec((seq, None, own, rows, cols), lambda c: (0, part, 0, 0, c)),
        out_shape=in_hbm((seq, parts, own, rows, channels)),
        input_output_aliases={} if buffer is None else {2: 0},
        compiler_params=params(0),
        name="second",
    )(weight, five, *(() if buffer is None else (buffer.reshape(seq, parts, own, rows, channels),)))
    return out.reshape(seq, parts, height, channels)


def spread_store(values, own_ref, send_ref):
    for half, ref in ((0, own_ref), (1, send_ref)):
        parts = [v[:, half * LANES : (half + 1) * LANES] for v in values]
        for g, part in enumerate(swap_lanes(parts)):
            ref[g] = part.astype(BF)


def gather_load(own_ref, recv_ref):
    own = swap_lanes([own_ref[g].astype(F32) for g in range(own_ref.shape[0])])
    recv = swap_lanes([recv_ref[g].astype(F32) for g in range(recv_ref.shape[0])])
    return [jnp.concatenate([a, b], axis=1).astype(BF) for a, b in zip(own, recv)]


def offset_call(kernel, chunk, steps, in_specs, out_specs, out_shape, aliases=None, scratch=()):
    call = pl.pallas_call(
        lambda _, *refs: kernel(*refs),
        grid_spec=pltpu.PrefetchScalarGridSpec(
            num_scalar_prefetch=1,
            grid=(steps,),
            in_specs=in_specs,
            out_specs=out_specs,
            scratch_shapes=scratch,
        ),
        out_shape=out_shape,
        input_output_aliases={k + 1: v for k, v in (aliases or {}).items()},
        compiler_params=params(0),
    )
    return functools.partial(call, jnp.stack([jnp.int32(v) for v in chunk]))


def natural_block(rows, steps, channels):
    return pl.BlockSpec((rows, rows, channels), lambda s, chunk: (0, chunk[0] * steps + s, 0))


def back_kernel(g_ref, w_ref, own_ref, send_ref):
    rows, cols, channels = g_ref.shape
    grad = g_ref[...].reshape(rows * cols, channels)
    blocks, width = w_ref.shape[0], w_ref.shape[2]
    values = [dot_nt(grad[:, h * width : (h + 1) * width], w_ref[h]) for h in range(blocks)]
    spread_store(values, own_ref, send_ref)


def back_stage(g3, down_second):
    rows, length, channels = g3.shape
    size = rows * rows
    blocks = down_second.shape[0]
    shape = jax.ShapeDtypeStruct((blocks, rows * length, LANES), BF)
    spec = pl.BlockSpec((blocks, size, LANES), lambda s: (0, s, 0))
    return pl.pallas_call(
        back_kernel,
        grid=(length // rows,),
        in_specs=[pl.BlockSpec((rows, rows, channels), lambda s: (0, s, 0)), full(down_second.shape)],
        out_specs=[spec, spec],
        out_shape=[shape, shape],
        compiler_params=params(0),
        name="back",
    )(g3, down_second)


def hidden_kernel(x_ref, m_ref, w_ref, h_ref, own_ref, send_ref):
    rows, cols, channels = x_ref.shape
    mixed = dot(swap_rows(rows), m_ref[...].reshape(rows * cols, channels))
    inputs = x_ref[...].reshape(rows * cols, channels).astype(F32)
    hidden = (inputs + jax.nn.sigmoid(inputs) * mixed).astype(BF)
    h_ref[...] = hidden
    blocks, width = w_ref.shape[0], w_ref.shape[1]
    values = [dot(hidden[:, k * width : (k + 1) * width], w_ref[k]) for k in range(blocks)]
    spread_store(values, own_ref, send_ref)


def arriving(field, size):
    source, part = field
    height, channels = source.shape[2:]
    return pl.BlockSpec((size // height, None, height, channels), lambda s, *_: (s, part, 0, 0))


def hidden_stage(chunk, x3, mixed, up_first):
    rows, length, channels = x3.shape
    size = rows * rows
    steps = length // CHUNKS // rows
    blocks = up_first.shape[0]
    part = pl.BlockSpec((blocks, size, LANES), lambda s, _: (0, s, 0))
    return offset_call(
        hidden_kernel,
        (chunk,),
        steps,
        [natural_block(rows, steps, channels), arriving(mixed, size), full(up_first.shape)],
        [pl.BlockSpec((size, channels), lambda s, _: (s, 0)), part, part],
        [
            jax.ShapeDtypeStruct((steps * size, channels), BF),
            jax.ShapeDtypeStruct((blocks, steps * size, LANES), BF),
            in_hbm((blocks, steps * size, LANES)),
        ],
    )(x3, mixed[0], up_first)


def middle_kernel(cols, *refs):
    uo, ur, bo, br, us, df, sus_in, sdf_in = refs[:8]
    down_own, down_send, grad_own, grad_send, sus, sdf = refs[8:]
    start = pl.program_id(1) == 0

    @pl.when(start)
    def _():
        sus[...] = sus_in[...]
        sdf[...] = sdf_in[...]

    up = jnp.concatenate([uo[0], ur[0]], axis=1)
    back = jnp.concatenate([bo[0], br[0]], axis=1)
    hidden_units = us.shape[2]
    down = None
    grad = None
    for low in range(0, hidden_units, cols):
        part = slice(low, low + cols)
        z = dot(up, us[0, :, part])
        z2 = z * z
        h = 0.5 + 0.5 * jnp.tanh(z * (root_two_pi + (root_two_pi * cubic_term) * z2))
        act = (z * h).astype(BF)
        slope = h + (h - h * h) * (
            z * (2.0 * root_two_pi + (6.0 * root_two_pi * cubic_term) * z2)
        )
        pre = (dot_nt(back, df[0, part, :]) * slope).astype(BF)
        step = dot(act, df[0, part, :])
        down = step if down is None else down + step
        step = dot_nt(pre, us[0, :, part])
        grad = step if grad is None else grad + step
        sdf[0, part, :] += dot_tn(act, back)
        sus[0, :, part] += dot_tn(up, pre)
    down_own[0] = down[:, :LANES].astype(BF)
    down_send[0] = down[:, LANES:].astype(BF)
    grad_own[0] = grad[:, :LANES].astype(BF)
    grad_send[0] = grad[:, LANES:].astype(BF)


def middle_stage(chunk, up_own, up_recv, back_own, back_recv, up_second, down_first, sums, tile=512, cols=256):
    blocks, count, _ = up_own.shape
    steps = count // tile
    part = pl.BlockSpec((1, tile, LANES), lambda g, t: (g, t, 0))
    shifted = pl.BlockSpec((1, tile, LANES), lambda g, t: (g, chunk * steps + t, 0))
    us_spec = pl.BlockSpec((1,) + up_second.shape[1:], lambda g, t: (g, 0, 0))
    df_spec = pl.BlockSpec((1,) + down_first.shape[1:], lambda g, t: (g, 0, 0))
    shape = jax.ShapeDtypeStruct(up_own.shape, BF)
    return pl.pallas_call(
        functools.partial(middle_kernel, cols),
        grid=(blocks, steps),
        in_specs=[part, part, shifted, shifted, us_spec, df_spec, us_spec, df_spec],
        out_specs=[part] * 4 + [us_spec, df_spec],
        out_shape=[shape] * 4
        + [jax.ShapeDtypeStruct(up_second.shape, F32), jax.ShapeDtypeStruct(down_first.shape, F32)],
        input_output_aliases={6: 4, 7: 5},
        compiler_params=params(0, 0),
        name="middle",
    )(up_own, up_recv, back_own, back_recv, up_second, down_first, *sums)


def input_kernel(*refs):
    x_ref, g_ref, m_ref, h_ref, go, gr, w_ref, suf_in = refs[:8]
    send_ref, base_ref, suf = refs[-3:]

    @pl.when(pl.program_id(0) == 0)
    def _():
        suf[...] = suf_in[...]

    rows, cols, channels = x_ref.shape
    size = rows * cols
    swap = swap_rows(rows)
    width = w_ref.shape[1]
    mids = gather_load(go, gr)
    x3, g3 = x_ref[...].reshape(size, channels), g_ref[...].reshape(size, channels)
    for k, mid in enumerate(mids):
        part = slice(k * width, (k + 1) * width)
        inner = dot_nt(mid, w_ref[k])
        suf[k] += dot_tn(h_ref[:, part], mid)
        grad = (g3[:, part].astype(F32) + inner).astype(BF).astype(F32)
        gating = jax.nn.sigmoid(x3[:, part].astype(F32))
        mixed = dot(swap, m_ref[:, :, part].reshape(size, width))
        send = dot(swap, (grad * gating).astype(BF)).astype(BF)
        send_ref[:, :, part] = send.reshape(send_ref.shape[0], send_ref.shape[1], width)
        base_ref[:, part] = (grad * (1.0 + gating * (1.0 - gating) * mixed)).astype(BF)


def input_stage(chunk, x3, g3, mixed, hidden, grad_own, grad_recv, up_first, sums, place, buffer):
    rows, length, channels = x3.shape
    size = rows * rows
    steps = length // CHUNKS // rows
    blocks = up_first.shape[0]
    flat = pl.BlockSpec((size, channels), lambda s, _: (s, 0))
    half = pl.BlockSpec((blocks, size, LANES), lambda s, _: (0, s, 0))
    natural = natural_block(rows, steps, channels)
    wspec = full(up_first.shape)
    seq, _, height, _ = mixed[0].shape
    part, parts = place
    return offset_call(
        input_kernel,
        (chunk, part),
        steps,
        [natural, natural, arriving(mixed, size), flat, half, half, wspec, wspec, pl.BlockSpec(memory_space=pl.ANY)],
        [
            pl.BlockSpec((size // height, None, height, channels), lambda s, at: (s, at[1], 0, 0)),
            flat,
            wspec,
        ],
        [
            in_hbm((seq, parts, height, channels)),
            jax.ShapeDtypeStruct((steps * size, channels), BF),
            jax.ShapeDtypeStruct(up_first.shape, F32),
        ],
        {7: 2, 8: 0},
    )(x3, g3, mixed[0], hidden, grad_own, grad_recv, up_first, sums, buffer)


def output_kernel(fresh, *refs):
    g_ref, h_ref, do, dr, w_ref = refs[:5]
    refs = refs[5:]
    if not fresh:
        sds_in = refs[0]
        refs = refs[2:]
    o_ref, sds, perms = refs

    @pl.when(pl.program_id(0) == 0)
    def _():
        sds[...] = jnp.zeros(sds.shape, F32) if fresh else sds_in[...]

    rows, cols, _ = g_ref.shape
    size = rows * cols
    width = w_ref.shape[2]
    for h, perm in enumerate(gather_load(do, dr)):
        perms[h] = perm

    @pl.loop(0, w_ref.shape[0])
    def _(h):
        part = pl.ds(pl.multiple_of(h * width, width), width)
        perm = perms[h]
        value = h_ref[:, part].astype(F32) + dot(perm, w_ref[h])
        o_ref[:, :, part] = value.astype(BF).reshape(rows, cols, width)
        sds[h] += dot_tn(perm, g_ref[:, :, part].reshape(size, width))


def output_stage(chunk, g3, hidden, down_own, down_recv, down_second, sums, output):
    rows, length, channels = g3.shape
    size = rows * rows
    steps = length // CHUNKS // rows
    blocks = down_second.shape[0]
    flat = pl.BlockSpec((size, channels), lambda s, _: (s, 0))
    part = pl.BlockSpec((blocks, size, LANES), lambda s, _: (0, s, 0))
    natural = natural_block(rows, steps, channels)
    fresh = sums is None
    wspec = full(down_second.shape)
    return offset_call(
        functools.partial(output_kernel, fresh),
        (chunk,),
        steps,
        [natural, flat, part, part, wspec] + ([] if fresh else [wspec, pl.BlockSpec(memory_space=pl.ANY)]),
        [natural, wspec],
        [jax.ShapeDtypeStruct(g3.shape, BF), jax.ShapeDtypeStruct(down_second.shape, F32)],
        {} if fresh else {5: 1, 6: 0},
        [pltpu.VMEM((blocks, size, 2 * LANES), BF)],
    )(g3, hidden, down_own, down_recv, down_second, *(() if fresh else (sums, output)))


def last_kernel(rows, w_ref, tw_ref, *refs):
    chunk_refs, base_refs = refs[:CHUNKS], refs[CHUNKS : 2 * CHUNKS]
    o_ref, scratch = refs[2 * CHUNKS :]
    size = rows * rows
    swap = swap_rows(rows)
    cols = o_ref.shape[2]
    height = chunk_refs[0].shape[1]
    count = size // height
    groups = chunk_refs[0].shape[0] // count
    for n, ref in enumerate(chunk_refs):
        for g in range(groups):
            index = n * groups + g
            piece = ref[g * count : (g + 1) * count].reshape(size, cols)
            value = dot(swap, piece) * tw_ref[:, index : index + 1]
            scratch[:, index * rows : (index + 1) * rows, :] = value.astype(BF).reshape(rows, rows, cols)
    weight = w_ref[...]
    for a in range(rows):
        base = jnp.concatenate(
            [ref[g * size + a * rows : g * size + (a + 1) * rows, :] for ref in base_refs for g in range(groups)],
            axis=0,
        )
        o_ref[a] = (dot(weight, scratch[a]) + base.astype(F32)).astype(BF)


def last_stage(rows, length, mix_first, tw_cols, fields, bases, cols=256):
    seq, _, height, channels = fields[0][0].shape
    spec = pl.BlockSpec((bases[0].shape[0], cols), lambda c: (0, c))
    field_specs = [
        pl.BlockSpec((seq, None, height, cols), lambda c, part=part: (0, part, 0, c)) for _, part in fields
    ]
    return pl.pallas_call(
        functools.partial(last_kernel, rows),
        grid=(channels // cols,),
        in_specs=[full(mix_first.shape), full(tw_cols.shape)] + field_specs + [spec] * CHUNKS,
        out_specs=pl.BlockSpec((rows, length, cols), lambda c: (0, 0, c)),
        out_shape=jax.ShapeDtypeStruct((rows, length, channels), BF),
        scratch_shapes=[pltpu.VMEM((rows, length, cols), BF)],
        compiler_params=params(0),
        name="last",
    )(mix_first, tw_cols, *[f for f, _ in fields], *bases)


def group_matrix(mine, width, blocks):
    stride = width // NBLK
    out = lax.broadcasted_iota(jnp.int32, (width, width), 0)
    inp = lax.broadcasted_iota(jnp.int32, (width, width), 1)
    k = inp % NBLK
    half = k // blocks
    half = half + mine - 2 * half * mine
    target = half * LANES + (k % blocks) * stride + inp // NBLK
    return jnp.where(out == target, 1.0, 0.0).astype(BF)


def copy_halves(mine, source, targets):
    for own in range(2):

        @pl.when(mine == own)
        def _():
            for get, put, kind in zip(source, targets, [t[0].dtype for t in targets]):
                value = get()
                low, high = value[..., :LANES], value[..., LANES:]
                ref, index = put
                ref[(*index, slice(0, LANES))] = (high if own else low).astype(kind)
                ref[(*index, slice(LANES, 2 * LANES))] = (low if own else high).astype(kind)


def prepare_kernel(mine_ref, uf, us, df, ds, uf_out, us_out, df_out, ds_out, *sums):
    for ref in sums:
        ref[...] = jnp.zeros(ref.shape, F32)
    mine = mine_ref[0]
    matrix = group_matrix(mine, ds.shape[1], NBLK // 2)
    copy_halves(mine, (lambda: uf[0], lambda: df[0]), ((uf_out, (0, slice(None))), (df_out, (0, slice(None)))))
    us_out[0] = dot(matrix, us[0]).astype(BF)
    ds_out[0] = dot(matrix, ds[0]).astype(BF)


def by_block(array):
    return pl.BlockSpec((1,) + array.shape[1:], lambda g, *_: (g, 0, 0))


def prepare_stage(mine, weights):
    specs = [by_block(w) for w in weights]
    return pl.pallas_call(
        prepare_kernel,
        grid_spec=pltpu.PrefetchScalarGridSpec(
            num_scalar_prefetch=1,
            grid=(weights[0].shape[0],),
            in_specs=specs,
            out_specs=specs + specs[:3],
        ),
        out_shape=[jax.ShapeDtypeStruct(w.shape, BF) for w in weights]
        + [jax.ShapeDtypeStruct(w.shape, F32) for w in weights[:3]],
        compiler_params=params(0),
        name="prepare",
    )(mine, *weights)


def collect_kernel(scale, width, *refs):
    out, row = refs[-1], 0
    for ref in refs[:-1]:
        for low in range(0, ref.shape[2], width):
            out[0, row : row + ref.shape[1], :] = (ref[0, :, low : low + width] * scale).astype(BF)
            row += ref.shape[1]


def collect_stage(scale, width, sums):
    blocks = sums[0].shape[0]
    height = sum(v.shape[1] * v.shape[2] for v in sums) // width
    return pl.pallas_call(
        functools.partial(collect_kernel, scale, width),
        grid=(blocks,),
        in_specs=[by_block(v) for v in sums],
        out_specs=pl.BlockSpec((1, height, width), lambda g: (g, 0, 0)),
        out_shape=jax.ShapeDtypeStruct((blocks, height, width), BF),
        compiler_params=params(0),
        name="collect",
    )(*sums)


def finish_kernel(mine_ref, large, small, uf, us, df, ds):
    mine = mine_ref[0]
    width = ds.shape[1]
    matrix = group_matrix(mine, width, NBLK // 2)
    for low in range(0, us.shape[2], width):
        us[0, :, low : low + width] = dot_tn(matrix, large[0, low : low + width, :])
    row = us.shape[2]
    copy_halves(
        mine,
        (lambda: large[0, row : row + df.shape[1], :], lambda: small[0, :width, :]),
        ((df, (0, slice(None))), (uf, (0, slice(None)))),
    )
    ds[0] = dot_tn(matrix, small[0, width : 2 * width, :])


def finish_stage(mine, wholes, weights):
    specs = [by_block(w) for w in weights]
    return pl.pallas_call(
        finish_kernel,
        grid_spec=pltpu.PrefetchScalarGridSpec(
            num_scalar_prefetch=1,
            grid=(wholes[0].shape[0],),
            in_specs=[by_block(v) for v in wholes],
            out_specs=specs,
        ),
        out_shape=[jax.ShapeDtypeStruct(w.shape, F32) for w in weights],
        compiler_params=params(0),
        name="finish",
    )(mine, *wholes)


def exchange(field):
    return lax.all_to_all(field, "seq", split_axis=0, concat_axis=0, tiled=True)


def partner(values):
    return lax.ppermute(values, "fsdp", [(0, 1), (1, 0)])


PLAN = (
    (((1, 0),), (("first", 1), ("prepare", 0), ("back", 0))),
    (((1, 1),), (("second", 0),)),
    (((2, 0), (1, 2)), (("second", 1),)),
    (((2, 1), (1, 3)), (("hidden", 0), ("second", 2), ("middle", 0), ("inputs", 0))),
    (((2, 2), (3, 0)), (("hidden", 1), ("second", 3), ("middle", 1), ("outputs", 0), ("inputs", 1))),
    (((2, 3), (3, 1)), (("hidden", 2), ("fourth", 0), ("middle", 2), ("outputs", 1), ("inputs", 2))),
    (((3, 2), (4, 0)), (("hidden", 3), ("fourth", 1), ("middle", 3), ("collect", 0), ("outputs", 2), ("inputs", 3))),
    (((3, 3), (4, 1)), (("fourth", 2), ("outputs", 3), ("collect", 1))),
    (((4, 2),), (("fourth", 3),)),
    (((4, 3),), (("finish", 0),)),
)


def tie(value, others):
    return lax.optimization_barrier((value, others))[0]


def chunked_shards(
    seq,
    activations,
    mix_first,
    twiddle,
    mix_second,
    up_first,
    up_second,
    down_first,
    down_second,
    grad_out,
):
    local_rows, channels = activations.shape
    rows, length = twiddle.shape
    mine = lax.axis_index("fsdp").astype(jnp.int32).reshape(1)
    weights = (up_first, up_second, down_first, down_second)

    x3 = activations.reshape(rows, length, channels)
    g3 = grad_out.reshape(rows, length, channels)
    w2, w2t = mix_second, mix_second.T
    tw_cols = jnp.transpose(twiddle.reshape(rows, length // rows, rows), (0, 2, 1)).reshape(
        rows * rows, length // rows
    )

    place = {}
    for slot, (travels, _) in enumerate(PLAN):
        for part, key in enumerate(travels):
            place[key] = (slot, part, len(travels))
    buffers, arrived, kept = {}, {}, {}
    halves = [list(range(seq // 2)), list(range(seq // 2, seq))]
    sum_last, output = None, None

    def spot(key):
        slot, part, parts = place[key]
        return (part, parts), buffers.get(slot)

    def first(chunks):
        results = first_stage(chunks, [place[1, m][1:] for m in chunks], seq, x3, mix_first, twiddle)
        for m, sent in zip(chunks, results):
            buffers[place[1, m][0]] = sent

    first((0,))
    ups_first, ups_second, downs_first, downs_second, sum_first, *sums = prepare_stage(mine, weights)
    for slot, (travels, tasks) in enumerate(PLAN):
        done = exchange(buffers[slot])
        for part, key in enumerate(travels):
            arrived[key] = (done, part)
        for name, n in tasks:
            if name == "first":
                first(tuple(range(1, CHUNKS)))
            elif name == "back":
                own, send = back_stage(g3, downs_second)
                back = (own, partner(send))
            elif name == "second":
                buffers[place[2, n][0]] = second_stage(w2t, arrived[1, n], *spot((2, n)), rows)
            elif name == "hidden":
                hidden, own, send = hidden_stage(n, x3, arrived[2, n], ups_first)
                kept["hidden", n] = hidden
                kept["up", n] = (own, partner(send))
            elif name == "middle":
                down_own, down_send, grad_own, grad_send, *sums = middle_stage(
                    n, *kept["up", n], *back, ups_second, downs_first, sums
                )
                kept["grad", n] = (grad_own, partner(grad_send))
                kept["down", n] = (down_own, partner(down_send))
            elif name == "inputs":
                buffers[place[3, n][0]], kept["base", n], sum_first = input_stage(
                    n,
                    x3,
                    g3,
                    arrived[2, n],
                    kept["hidden", n],
                    *kept["grad", n],
                    ups_first,
                    sum_first,
                    *spot((3, n)),
                )
            elif name == "outputs":
                output, sum_last = output_stage(
                    n, g3, kept["hidden", n], *kept["down", n], downs_second, sum_last, output
                )
            elif name == "fourth":
                buffers[place[4, n][0]] = second_stage(w2, arrived[3, n], *spot((4, n)), rows)

    width = up_first.shape[1]
    after = (buffers[place[4, CHUNKS - 1][0]], arrived[4, CHUNKS - 2][0])
    wholes = []
    for n, values in enumerate((sums, (sum_first, sum_last))):
        collected = collect_stage(1.0 / length, width, values)
        part = lax.psum_scatter(
            collected.reshape(-1, width), "seq", scatter_dimension=0, axis_index_groups=halves, tiled=True
        )
        other = lax.ppermute(part, "seq", [(d, (d + seq // 2) % seq) for d in range(seq)])
        other = tie(other, after[n])
        part = (part.astype(F32) + other.astype(F32)).astype(BF)
        whole = lax.all_gather(part, "seq", axis=0, axis_index_groups=halves, tiled=True)
        wholes.append(whole.reshape(collected.shape))
    grads = finish_stage(mine, wholes, weights)
    tw_cols = tie(tw_cols, grads)
    fields = [arrived[4, n] for n in range(CHUNKS)]
    bases = [kept["base", n] for n in range(CHUNKS)]
    grad_inputs = last_stage(rows, length, mix_first, tw_cols, fields, bases)
    return (
        output.reshape(local_rows, channels),
        grad_inputs.reshape(local_rows, channels),
        *grads,
    )


def shards(*args):
    _, _, twiddle, _, up_first = args[:5]
    rows, length = twiddle.shape
    blocks, width = up_first.shape[0], up_first.shape[1]
    seq = length // rows
    fits = (
        blocks * (width // NBLK) == LANES
        and 2 * blocks == NBLK
        and rows == 16
        and seq == 16
        and length % (CHUNKS * seq) == 0
    )
    if fits:
        return chunked_shards(seq, *args)
    return general_shards(*args)


def solution(mesh):
    in_specs = (
        P("seq", "fsdp"),
        P(),
        P("seq", None),
        P(),
        P("fsdp", None, None),
        P("fsdp", None, None),
        P("fsdp", None, None),
        P("fsdp", None, None),
        P("seq", "fsdp"),
    )
    out_specs = (
        P("seq", "fsdp"),
        P("seq", "fsdp"),
        P("fsdp", None, None),
        P("fsdp", None, None),
        P("fsdp", None, None),
        P("fsdp", None, None),
    )
    return jax.shard_map(shards, mesh=mesh, in_specs=in_specs, out_specs=out_specs, check_vma=False)
```

```python
import functools

import jax
import jax.numpy as jnp
from jax import lax
from jax.experimental import pallas as pl
from jax.experimental.pallas import tpu as pltpu
from jax.sharding import PartitionSpec as P


FIRST = "first"
PREPARE = "prepare"
BACK = "back"
SECOND = "second"
HIDDEN = "hidden"
MIDDLE = "middle"
INPUTS = "inputs"
OUTPUTS = "outputs"
FOURTH = "fourth"
COLLECT = "collect"
FINISH = "finish"
UP = "up"
GRAD = "grad"
DOWN = "down"
SEQ = "seq"
FSDP = "fsdp"
BASE = "base"
NBLK = 8
LANES = 128
CHUNKS = 4


root_two_pi = 0.7978845608028654
cubic_term = 0.044715

BF = jnp.bfloat16
F32 = jnp.float32


def gelu_value(values):
    inner = root_two_pi * (values + cubic_term * values * values * values)
    return 0.5 * values * (1.0 + jnp.tanh(inner))


def gelu_slope(values):
    inner = root_two_pi * (values + cubic_term * values * values * values)
    hyper = jnp.tanh(inner)
    return 0.5 * (1.0 + hyper) + 0.5 * values * (1.0 - hyper * hyper) * root_two_pi * (
        1.0 + 3.0 * cubic_term * values * values
    )


def product(form, left, right):
    return jnp.einsum(form, left, right, preferred_element_type=jnp.float32)


def column_pass(field, factor):
    result = product(
        "ajc,ai->ijc", lax.all_to_all(field, SEQ, split_axis=1, concat_axis=0, tiled=True), factor
    ).astype(jnp.bfloat16)
    return lax.all_to_all(result, SEQ, split_axis=0, concat_axis=1, tiled=True)


def shuffle_blocks(values):
    return lax.all_to_all(values, FSDP, split_axis=2, concat_axis=1, tiled=True)


def spread_blocks(values):
    count, local_blocks, width = values.shape
    stride = width // NBLK
    received = shuffle_blocks(values)
    shaped = received.reshape(count, NBLK, local_blocks, stride)
    return jnp.transpose(shaped, (0, 2, 3, 1)).reshape(count, local_blocks, width)


def return_blocks(values):
    count, local_blocks, width = values.shape
    stride = width // NBLK
    parts = NBLK // local_blocks
    shaped = values.reshape(count, local_blocks, stride, parts, local_blocks)
    sending = jnp.transpose(shaped, (0, 1, 3, 4, 2)).reshape(count, local_blocks, width)
    received = shuffle_blocks(sending).reshape(count, NBLK, local_blocks, stride)
    return jnp.transpose(received, (0, 2, 1, 3)).reshape(count, local_blocks, width)


def blocks_layer(hidden, grad_out, up_first, up_second, down_first, down_second):
    count, channels = hidden.shape
    local_blocks, width = (up_first.shape[0], up_first.shape[1])
    hidden_three = hidden.reshape(count, local_blocks, width)
    up_mid = product("tkp,kpq->tkq", hidden_three, up_first).astype(jnp.bfloat16)
    up_perm = spread_blocks(up_mid)
    pre_act = product("tge,geo->tgo", up_perm, up_second)
    activated = gelu_value(pre_act).astype(jnp.bfloat16)
    down_mid = product("tgo,goq->tgq", activated, down_first).astype(jnp.bfloat16)
    down_perm = spread_blocks(down_mid)
    down_out = product("tge,geq->tgq", down_perm, down_second).reshape(count, channels)
    output = (hidden.astype(jnp.float32) + down_out).astype(jnp.bfloat16)
    grad_three = grad_out.reshape(count, local_blocks, width)
    sum_down_second = product("tge,tgq->geq", down_perm, grad_three)
    back_perm = product("tgq,geq->tge", grad_three, down_second).astype(jnp.bfloat16)
    back_mid = return_blocks(back_perm)
    sum_down_first = product("tgo,tgq->goq", activated, back_mid)
    grad_act = product("tgq,goq->tgo", back_mid, down_first)
    grad_pre = (grad_act * gelu_slope(pre_act)).astype(jnp.bfloat16)
    sum_up_second = product("tge,tgo->geo", up_perm, grad_pre)
    grad_perm = product("tgo,geo->tge", grad_pre, up_second).astype(jnp.bfloat16)
    grad_mid = return_blocks(grad_perm)
    sum_up_first = product("tkp,tkq->kpq", hidden_three, grad_mid)
    grad_inner = product("tkq,kpq->tkp", grad_mid, up_first).reshape(count, channels)
    grad_hidden = (grad_out.astype(jnp.float32) + grad_inner).astype(jnp.bfloat16)
    return (output, grad_hidden, (sum_up_first, sum_up_second, sum_down_first, sum_down_second))


def general_shards(
    activations,
    mix_first,
    twiddle,
    mix_second,
    up_first,
    up_second,
    down_first,
    down_second,
    grad_out,
):
    local_rows, local_channels = activations.shape
    block_rows = twiddle.shape[0]
    length = mix_first.shape[0]
    inputs_three = activations.reshape(block_rows, length, local_channels)
    first_pass = (product("abc,bj->ajc", inputs_three, mix_first) * twiddle[:, :, None]).astype(
        jnp.bfloat16
    )
    mixed = column_pass(first_pass, mix_second).reshape(local_rows, local_channels)
    inputs_float = activations.astype(jnp.float32)
    gating = jax.nn.sigmoid(inputs_float)
    mixed_float = mixed.astype(jnp.float32)
    hidden = (inputs_float + gating * mixed_float).astype(jnp.bfloat16)
    output, grad_hidden, grads = blocks_layer(
        hidden, grad_out, up_first, up_second, down_first, down_second
    )
    totals = lax.psum((grads[0], grads[1], grads[2], grads[3]), SEQ)
    grad_float = grad_hidden.astype(jnp.float32)
    grad_mixed = (grad_float * gating).astype(jnp.bfloat16)
    back_rows = column_pass(grad_mixed.reshape(block_rows, length, local_channels), mix_second.T)
    twisted = (back_rows.astype(jnp.float32) * twiddle[:, :, None]).astype(jnp.bfloat16)
    mix_grad = product("ajc,bj->abc", twisted, mix_first).reshape(local_rows, local_channels)
    grad_inputs = (grad_float * (1.0 + gating * (1.0 - gating) * mixed_float) + mix_grad).astype(
        jnp.bfloat16
    )
    scale = 1.0 / length
    return (
        output,
        grad_inputs,
        totals[0] * scale,
        totals[1] * scale,
        totals[2] * scale,
        totals[3] * scale,
    )


def dot(left, right):
    return jnp.dot(left, right, preferred_element_type=F32)


def dot_nt(left, right):
    return lax.dot_general(left, right, (((1,), (1,)), ((), ())), preferred_element_type=F32)


def dot_tn(left, right):
    return lax.dot_general(left, right, (((0,), (0,)), ((), ())), preferred_element_type=F32)


def swap_rows(rows):
    size = rows * rows
    out = lax.broadcasted_iota(jnp.int32, (size, size), 0)
    inp = lax.broadcasted_iota(jnp.int32, (size, size), 1)
    same = (out // rows == inp % rows) & (out % rows == inp // rows)
    return jnp.where(same, 1.0, 0.0).astype(BF)


def swap_lanes(parts):
    lane = lax.broadcasted_iota(jnp.int32, parts[0].shape, 1)
    low = lane < 64
    even = (lane & 32) == 0
    x0, x1, x2, x3 = parts
    a0 = jnp.where(low, x0, pltpu.roll(x2, 64, 1))
    a2 = jnp.where(low, pltpu.roll(x0, 64, 1), x2)
    a1 = jnp.where(low, x1, pltpu.roll(x3, 64, 1))
    a3 = jnp.where(low, pltpu.roll(x1, 64, 1), x3)
    b0 = jnp.where(even, a0, pltpu.roll(a1, 32, 1))
    b1 = jnp.where(even, pltpu.roll(a0, 96, 1), a1)
    b2 = jnp.where(even, a2, pltpu.roll(a3, 32, 1))
    b3 = jnp.where(even, pltpu.roll(a2, 96, 1), a3)
    return b0, b1, b2, b3


def params(*semantics):
    return pltpu.CompilerParams(
        dimension_semantics=("arbitrary",) * len(semantics), vmem_limit_bytes=58 * 1024 * 1024
    )


def in_hbm(shape, kind=BF):
    return jax.ShapeDtypeStruct(shape, kind)


def full(shape):
    zeros = (0,) * len(shape)
    return pl.BlockSpec(shape, lambda *_: zeros)


def first_kernel(chunks, span, rows, x_ref, w_ref, tw_ref, *rest):
    outs, scratch = rest[: len(chunks)], rest[len(chunks)]
    swap = swap_rows(rows)
    low, high = chunks[0] * span, (chunks[-1] + 1) * span
    weight = w_ref[...].T[low:high, :]
    scales = tw_ref[...].T[low:high, :]
    for a in range(rows):
        value = dot(weight, x_ref[a]) * scales[:, a : a + 1]
        scratch[a] = value.astype(BF)
    size = rows * rows
    for n, out in enumerate(outs):
        _, _, height, cols = out.shape
        count = size // height
        for group in range(span // rows):
            start = n * span + group * rows
            piece = scratch[:, start : start + rows, :].reshape(size, cols)
            value = dot(swap, piece).astype(BF)
            out[group * count : (group + 1) * count, 0] = value.reshape(count, height, cols)


def first_stage(chunks, places, seq, x3, mix_first, twiddle, cols=256):
    rows, length, channels = x3.shape
    span = length // CHUNKS
    height = span * rows // seq
    return pl.pallas_call(
        functools.partial(first_kernel, chunks, span, rows),
        grid=(channels // cols,),
        in_specs=[
            pl.BlockSpec((rows, length, cols), lambda c: (0, 0, c)),
            full(mix_first.shape),
            full(twiddle.shape),
        ],
        out_specs=[
            pl.BlockSpec((seq, 1, height, cols), lambda c, part=part: (0, part, 0, c)) for part, _ in places
        ],
        out_shape=[in_hbm((seq, parts, height, channels)) for _, parts in places],
        scratch_shapes=[pltpu.VMEM((rows, span * len(chunks), cols), BF)],
        compiler_params=params(0),
    )(x3, mix_first, twiddle)


def second_kernel(w_ref, x_ref, *refs):
    o_ref = refs[-1]
    seq, own, rows, cols = x_ref.shape
    weight = w_ref[...]
    for j in range(own):
        value = dot(weight, x_ref[:, j].reshape(seq * rows, cols))
        o_ref[:, j] = value.astype(BF).reshape(seq, rows, cols)


def second_stage(weight, field, place, buffer, rows, cols=256):
    source, part_in = field
    part, parts = place
    seq, parts_in, height, channels = source.shape
    own = height // rows
    five = source.reshape(seq, parts_in, own, rows, channels)
    out = pl.pallas_call(
        second_kernel,
        grid=(channels // cols,),
        in_specs=[
            full(weight.shape),
            pl.BlockSpec((seq, None, own, rows, cols), lambda c: (0, part_in, 0, 0, c)),
        ]
        + ([] if buffer is None else [pl.BlockSpec(memory_space=pl.ANY)]),
        out_specs=pl.BlockSpec((seq, None, own, rows, cols), lambda c: (0, part, 0, 0, c)),
        out_shape=in_hbm((seq, parts, own, rows, channels)),
        input_output_aliases={} if buffer is None else {2: 0},
        compiler_params=params(0),
    )(weight, five, *(() if buffer is None else (buffer.reshape(seq, parts, own, rows, channels),)))
    return out.reshape(seq, parts, height, channels)


def spread_store(values, own_ref, send_ref):
    for half, ref in ((0, own_ref), (1, send_ref)):
        parts = [v[:, half * LANES : (half + 1) * LANES] for v in values]
        for g, part in enumerate(swap_lanes(parts)):
            ref[g] = part.astype(BF)


def gather_load(own_ref, recv_ref):
    own = swap_lanes([own_ref[g].astype(F32) for g in range(own_ref.shape[0])])
    recv = swap_lanes([recv_ref[g].astype(F32) for g in range(recv_ref.shape[0])])
    return [jnp.concatenate([a, b], axis=1).astype(BF) for a, b in zip(own, recv)]


def offset_call(kernel, chunk, steps, in_specs, out_specs, out_shape, aliases=None, scratch=()):
    call = pl.pallas_call(
        lambda _, *refs: kernel(*refs),
        grid_spec=pltpu.PrefetchScalarGridSpec(
            num_scalar_prefetch=1,
            grid=(steps,),
            in_specs=in_specs,
            out_specs=out_specs,
            scratch_shapes=scratch,
        ),
        out_shape=out_shape,
        input_output_aliases={k + 1: v for k, v in (aliases or {}).items()},
        compiler_params=params(0),
    )
    return functools.partial(call, jnp.stack([jnp.int32(v) for v in chunk]))


def natural_block(rows, steps, channels):
    return pl.BlockSpec((rows, rows, channels), lambda s, chunk: (0, chunk[0] * steps + s, 0))


def back_kernel(g_ref, w_ref, own_ref, send_ref):
    rows, cols, channels = g_ref.shape
    grad = g_ref[...].reshape(rows * cols, channels)
    blocks, width = w_ref.shape[0], w_ref.shape[2]
    values = [dot_nt(grad[:, h * width : (h + 1) * width], w_ref[h]) for h in range(blocks)]
    spread_store(values, own_ref, send_ref)


def back_stage(g3, down_second):
    rows, length, channels = g3.shape
    size = rows * rows
    blocks = down_second.shape[0]
    shape = jax.ShapeDtypeStruct((blocks, rows * length, LANES), BF)
    spec = pl.BlockSpec((blocks, size, LANES), lambda s: (0, s, 0))
    return pl.pallas_call(
        back_kernel,
        grid=(length // rows,),
        in_specs=[pl.BlockSpec((rows, rows, channels), lambda s: (0, s, 0)), full(down_second.shape)],
        out_specs=[spec, spec],
        out_shape=[shape, shape],
        compiler_params=params(0),
    )(g3, down_second)


def hidden_kernel(x_ref, m_ref, w_ref, h_ref, own_ref, send_ref):
    rows, cols, channels = x_ref.shape
    mixed = dot(swap_rows(rows), m_ref[...].reshape(rows * cols, channels))
    inputs = x_ref[...].reshape(rows * cols, channels).astype(F32)
    hidden = (inputs + jax.nn.sigmoid(inputs) * mixed).astype(BF)
    h_ref[...] = hidden
    blocks, width = w_ref.shape[0], w_ref.shape[1]
    values = [dot(hidden[:, k * width : (k + 1) * width], w_ref[k]) for k in range(blocks)]
    spread_store(values, own_ref, send_ref)


def arriving(field, size):
    source, part = field
    height, channels = source.shape[2:]
    return pl.BlockSpec((size // height, None, height, channels), lambda s, *_: (s, part, 0, 0))


def hidden_stage(chunk, x3, mixed, up_first):
    rows, length, channels = x3.shape
    size = rows * rows
    steps = length // CHUNKS // rows
    blocks = up_first.shape[0]
    part = pl.BlockSpec((blocks, size, LANES), lambda s, _: (0, s, 0))
    return offset_call(
        hidden_kernel,
        (chunk,),
        steps,
        [natural_block(rows, steps, channels), arriving(mixed, size), full(up_first.shape)],
        [pl.BlockSpec((size, channels), lambda s, _: (s, 0)), part, part],
        [
            jax.ShapeDtypeStruct((steps * size, channels), BF),
            jax.ShapeDtypeStruct((blocks, steps * size, LANES), BF),
            in_hbm((blocks, steps * size, LANES)),
        ],
    )(x3, mixed[0], up_first)


def middle_kernel(cols, *refs):
    uo, ur, bo, br, us, df, sus_in, sdf_in = refs[:8]
    down_own, down_send, grad_own, grad_send, sus, sdf = refs[8:]
    start = pl.program_id(1) == 0

    @pl.when(start)
    def _():
        sus[...] = sus_in[...]
        sdf[...] = sdf_in[...]

    up = jnp.concatenate([uo[0], ur[0]], axis=1)
    back = jnp.concatenate([bo[0], br[0]], axis=1)
    hidden_units = us.shape[2]
    down = None
    grad = None
    for low in range(0, hidden_units, cols):
        part = slice(low, low + cols)
        z = dot(up, us[0, :, part])
        z2 = z * z
        h = 0.5 + 0.5 * jnp.tanh(z * (root_two_pi + (root_two_pi * cubic_term) * z2))
        act = (z * h).astype(BF)
        slope = h + (h - h * h) * (
            z * (2.0 * root_two_pi + (6.0 * root_two_pi * cubic_term) * z2)
        )
        pre = (dot_nt(back, df[0, part, :]) * slope).astype(BF)
        step = dot(act, df[0, part, :])
        down = step if down is None else down + step
        step = dot_nt(pre, us[0, :, part])
        grad = step if grad is None else grad + step
        sdf[0, part, :] += dot_tn(act, back)
        sus[0, :, part] += dot_tn(up, pre)
    down_own[0] = down[:, :LANES].astype(BF)
    down_send[0] = down[:, LANES:].astype(BF)
    grad_own[0] = grad[:, :LANES].astype(BF)
    grad_send[0] = grad[:, LANES:].astype(BF)


def middle_stage(chunk, up_own, up_recv, back_own, back_recv, up_second, down_first, sums, tile=512, cols=256):
    blocks, count, _ = up_own.shape
    steps = count // tile
    part = pl.BlockSpec((1, tile, LANES), lambda g, t: (g, t, 0))
    shifted = pl.BlockSpec((1, tile, LANES), lambda g, t: (g, chunk * steps + t, 0))
    us_spec = pl.BlockSpec((1,) + up_second.shape[1:], lambda g, t: (g, 0, 0))
    df_spec = pl.BlockSpec((1,) + down_first.shape[1:], lambda g, t: (g, 0, 0))
    shape = jax.ShapeDtypeStruct(up_own.shape, BF)
    return pl.pallas_call(
        functools.partial(middle_kernel, cols),
        grid=(blocks, steps),
        in_specs=[part, part, shifted, shifted, us_spec, df_spec, us_spec, df_spec],
        out_specs=[part] * 4 + [us_spec, df_spec],
        out_shape=[shape] * 4
        + [jax.ShapeDtypeStruct(up_second.shape, F32), jax.ShapeDtypeStruct(down_first.shape, F32)],
        input_output_aliases={6: 4, 7: 5},
        compiler_params=params(0, 0),
    )(up_own, up_recv, back_own, back_recv, up_second, down_first, *sums)


def input_kernel(*refs):
    x_ref, g_ref, m_ref, h_ref, go, gr, w_ref, suf_in = refs[:8]
    send_ref, base_ref, suf = refs[-3:]

    @pl.when(pl.program_id(0) == 0)
    def _():
        suf[...] = suf_in[...]

    rows, cols, channels = x_ref.shape
    size = rows * cols
    swap = swap_rows(rows)
    width = w_ref.shape[1]
    mids = gather_load(go, gr)
    x3, g3 = x_ref[...].reshape(size, channels), g_ref[...].reshape(size, channels)
    for k, mid in enumerate(mids):
        part = slice(k * width, (k + 1) * width)
        inner = dot_nt(mid, w_ref[k])
        suf[k] += dot_tn(h_ref[:, part], mid)
        grad = (g3[:, part].astype(F32) + inner).astype(BF).astype(F32)
        gating = jax.nn.sigmoid(x3[:, part].astype(F32))
        mixed = dot(swap, m_ref[:, :, part].reshape(size, width))
        send = dot(swap, (grad * gating).astype(BF)).astype(BF)
        send_ref[:, :, part] = send.reshape(send_ref.shape[0], send_ref.shape[1], width)
        base_ref[:, part] = (grad * (1.0 + gating * (1.0 - gating) * mixed)).astype(BF)


def input_stage(chunk, x3, g3, mixed, hidden, grad_own, grad_recv, up_first, sums, place, buffer):
    rows, length, channels = x3.shape
    size = rows * rows
    steps = length // CHUNKS // rows
    blocks = up_first.shape[0]
    flat = pl.BlockSpec((size, channels), lambda s, _: (s, 0))
    half = pl.BlockSpec((blocks, size, LANES), lambda s, _: (0, s, 0))
    natural = natural_block(rows, steps, channels)
    wspec = full(up_first.shape)
    seq, _, height, _ = mixed[0].shape
    part, parts = place
    return offset_call(
        input_kernel,
        (chunk, part),
        steps,
        [natural, natural, arriving(mixed, size), flat, half, half, wspec, wspec, pl.BlockSpec(memory_space=pl.ANY)],
        [
            pl.BlockSpec((size // height, None, height, channels), lambda s, at: (s, at[1], 0, 0)),
            flat,
            wspec,
        ],
        [
            in_hbm((seq, parts, height, channels)),
            jax.ShapeDtypeStruct((steps * size, channels), BF),
            jax.ShapeDtypeStruct(up_first.shape, F32),
        ],
        {7: 2, 8: 0},
    )(x3, g3, mixed[0], hidden, grad_own, grad_recv, up_first, sums, buffer)


def output_kernel(fresh, *refs):
    g_ref, h_ref, do, dr, w_ref = refs[:5]
    refs = refs[5:]
    if not fresh:
        sds_in = refs[0]
        refs = refs[2:]
    o_ref, sds, perms = refs

    @pl.when(pl.program_id(0) == 0)
    def _():
        sds[...] = jnp.zeros(sds.shape, F32) if fresh else sds_in[...]

    rows, cols, _ = g_ref.shape
    size = rows * cols
    width = w_ref.shape[2]
    for h, perm in enumerate(gather_load(do, dr)):
        perms[h] = perm

    @pl.loop(0, w_ref.shape[0])
    def _(h):
        part = pl.ds(pl.multiple_of(h * width, width), width)
        perm = perms[h]
        value = h_ref[:, part].astype(F32) + dot(perm, w_ref[h])
        o_ref[:, :, part] = value.astype(BF).reshape(rows, cols, width)
        sds[h] += dot_tn(perm, g_ref[:, :, part].reshape(size, width))


def output_stage(chunk, g3, hidden, down_own, down_recv, down_second, sums, output):
    rows, length, channels = g3.shape
    size = rows * rows
    steps = length // CHUNKS // rows
    blocks = down_second.shape[0]
    flat = pl.BlockSpec((size, channels), lambda s, _: (s, 0))
    part = pl.BlockSpec((blocks, size, LANES), lambda s, _: (0, s, 0))
    natural = natural_block(rows, steps, channels)
    fresh = sums is None
    wspec = full(down_second.shape)
    return offset_call(
        functools.partial(output_kernel, fresh),
        (chunk,),
        steps,
        [natural, flat, part, part, wspec] + ([] if fresh else [wspec, pl.BlockSpec(memory_space=pl.ANY)]),
        [natural, wspec],
        [jax.ShapeDtypeStruct(g3.shape, BF), jax.ShapeDtypeStruct(down_second.shape, F32)],
        {} if fresh else {5: 1, 6: 0},
        [pltpu.VMEM((blocks, size, 2 * LANES), BF)],
    )(g3, hidden, down_own, down_recv, down_second, *(() if fresh else (sums, output)))


def last_kernel(rows, w_ref, tw_ref, *refs):
    chunk_refs, base_refs = refs[:CHUNKS], refs[CHUNKS : 2 * CHUNKS]
    o_ref, scratch = refs[2 * CHUNKS :]
    size = rows * rows
    swap = swap_rows(rows)
    cols = o_ref.shape[2]
    height = chunk_refs[0].shape[1]
    count = size // height
    groups = chunk_refs[0].shape[0] // count
    for n, ref in enumerate(chunk_refs):
        for g in range(groups):
            index = n * groups + g
            piece = ref[g * count : (g + 1) * count].reshape(size, cols)
            value = dot(swap, piece) * tw_ref[:, index : index + 1]
            scratch[:, index * rows : (index + 1) * rows, :] = value.astype(BF).reshape(rows, rows, cols)
    weight = w_ref[...]
    for a in range(rows):
        base = jnp.concatenate(
            [ref[g * size + a * rows : g * size + (a + 1) * rows, :] for ref in base_refs for g in range(groups)],
            axis=0,
        )
        o_ref[a] = (dot(weight, scratch[a]) + base.astype(F32)).astype(BF)


def last_stage(rows, length, mix_first, tw_cols, fields, bases, cols=256):
    seq, _, height, channels = fields[0][0].shape
    spec = pl.BlockSpec((bases[0].shape[0], cols), lambda c: (0, c))
    field_specs = [
        pl.BlockSpec((seq, None, height, cols), lambda c, part=part: (0, part, 0, c)) for _, part in fields
    ]
    return pl.pallas_call(
        functools.partial(last_kernel, rows),
        grid=(channels // cols,),
        in_specs=[full(mix_first.shape), full(tw_cols.shape)] + field_specs + [spec] * CHUNKS,
        out_specs=pl.BlockSpec((rows, length, cols), lambda c: (0, 0, c)),
        out_shape=jax.ShapeDtypeStruct((rows, length, channels), BF),
        scratch_shapes=[pltpu.VMEM((rows, length, cols), BF)],
        compiler_params=params(0),
        name="last",
    )(mix_first, tw_cols, *[f for f, _ in fields], *bases)


def group_matrix(mine, width, blocks):
    stride = width // NBLK
    out = lax.broadcasted_iota(jnp.int32, (width, width), 0)
    inp = lax.broadcasted_iota(jnp.int32, (width, width), 1)
    k = inp % NBLK
    half = k // blocks
    half = half + mine - 2 * half * mine
    target = half * LANES + (k % blocks) * stride + inp // NBLK
    return jnp.where(out == target, 1.0, 0.0).astype(BF)


def copy_halves(mine, source, targets):
    for own in range(2):

        @pl.when(mine == own)
        def _():
            for get, put, kind in zip(source, targets, [t[0].dtype for t in targets]):
                value = get()
                low, high = value[..., :LANES], value[..., LANES:]
                ref, index = put
                ref[(*index, slice(0, LANES))] = (high if own else low).astype(kind)
                ref[(*index, slice(LANES, 2 * LANES))] = (low if own else high).astype(kind)


def prepare_kernel(mine_ref, uf, us, df, ds, uf_out, us_out, df_out, ds_out, *sums):
    for ref in sums:
        ref[...] = jnp.zeros(ref.shape, F32)
    mine = mine_ref[0]
    matrix = group_matrix(mine, ds.shape[1], NBLK // 2)
    copy_halves(mine, (lambda: uf[0], lambda: df[0]), ((uf_out, (0, slice(None))), (df_out, (0, slice(None)))))
    us_out[0] = dot(matrix, us[0]).astype(BF)
    ds_out[0] = dot(matrix, ds[0]).astype(BF)


def by_block(array):
    return pl.BlockSpec((1,) + array.shape[1:], lambda g, *_: (g, 0, 0))


def prepare_stage(mine, weights):
    specs = [by_block(w) for w in weights]
    return pl.pallas_call(
        prepare_kernel,
        grid_spec=pltpu.PrefetchScalarGridSpec(
            num_scalar_prefetch=1,
            grid=(weights[0].shape[0],),
            in_specs=specs,
            out_specs=specs + specs[:3],
        ),
        out_shape=[jax.ShapeDtypeStruct(w.shape, BF) for w in weights]
        + [jax.ShapeDtypeStruct(w.shape, F32) for w in weights[:3]],
        compiler_params=params(0),
    )(mine, *weights)


def collect_kernel(scale, width, *refs):
    out, row = refs[-1], 0
    for ref in refs[:-1]:
        for low in range(0, ref.shape[2], width):
            out[0, row : row + ref.shape[1], :] = (ref[0, :, low : low + width] * scale).astype(BF)
            row += ref.shape[1]


def collect_stage(scale, width, sums):
    blocks = sums[0].shape[0]
    height = sum(v.shape[1] * v.shape[2] for v in sums) // width
    return pl.pallas_call(
        functools.partial(collect_kernel, scale, width),
        grid=(blocks,),
        in_specs=[by_block(v) for v in sums],
        out_specs=pl.BlockSpec((1, height, width), lambda g: (g, 0, 0)),
        out_shape=jax.ShapeDtypeStruct((blocks, height, width), BF),
        compiler_params=params(0),
    )(*sums)


def finish_kernel(mine_ref, large, small, uf, us, df, ds):
    mine = mine_ref[0]
    width = ds.shape[1]
    matrix = group_matrix(mine, width, NBLK // 2)
    for low in range(0, us.shape[2], width):
        us[0, :, low : low + width] = dot_tn(matrix, large[0, low : low + width, :])
    row = us.shape[2]
    copy_halves(
        mine,
        (lambda: large[0, row : row + df.shape[1], :], lambda: small[0, :width, :]),
        ((df, (0, slice(None))), (uf, (0, slice(None)))),
    )
    ds[0] = dot_tn(matrix, small[0, width : 2 * width, :])


def finish_stage(mine, wholes, weights):
    specs = [by_block(w) for w in weights]
    return pl.pallas_call(
        finish_kernel,
        grid_spec=pltpu.PrefetchScalarGridSpec(
            num_scalar_prefetch=1,
            grid=(wholes[0].shape[0],),
            in_specs=[by_block(v) for v in wholes],
            out_specs=specs,
        ),
        out_shape=[jax.ShapeDtypeStruct(w.shape, F32) for w in weights],
        compiler_params=params(0),
    )(mine, *wholes)


def exchange(field):
    return lax.all_to_all(field, SEQ, split_axis=0, concat_axis=0, tiled=True)


def partner(values):
    return lax.ppermute(values, FSDP, [(0, 1), (1, 0)])


PLAN = (
    (((1, 0),), ((FIRST, 1), (PREPARE, 0), (BACK, 0))),
    (((1, 1),), ((SECOND, 0),)),
    (((2, 0), (1, 2)), ((SECOND, 1),)),
    (((2, 1), (1, 3)), ((HIDDEN, 0), (SECOND, 2), (MIDDLE, 0), (INPUTS, 0))),
    (((2, 2), (3, 0)), ((HIDDEN, 1), (SECOND, 3), (MIDDLE, 1), (OUTPUTS, 0), (INPUTS, 1))),
    (((2, 3), (3, 1)), ((HIDDEN, 2), (FOURTH, 0), (MIDDLE, 2), (OUTPUTS, 1), (INPUTS, 2))),
    (((3, 2), (4, 0)), ((HIDDEN, 3), (FOURTH, 1), (MIDDLE, 3), (COLLECT, 0), (OUTPUTS, 2), (INPUTS, 3))),
    (((3, 3), (4, 1)), ((FOURTH, 2), (OUTPUTS, 3), (COLLECT, 1))),
    (((4, 2),), ((FOURTH, 3),)),
    (((4, 3),), ((FINISH, 0),)),
)


def tie(value, others):
    return lax.optimization_barrier((value, others))[0]


def chunked_shards(
    seq,
    activations,
    mix_first,
    twiddle,
    mix_second,
    up_first,
    up_second,
    down_first,
    down_second,
    grad_out,
):
    local_rows, channels = activations.shape
    rows, length = twiddle.shape
    mine = lax.axis_index(FSDP).astype(jnp.int32).reshape(1)
    weights = (up_first, up_second, down_first, down_second)

    x3 = activations.reshape(rows, length, channels)
    g3 = grad_out.reshape(rows, length, channels)
    w2, w2t = mix_second, mix_second.T
    tw_cols = jnp.transpose(twiddle.reshape(rows, length // rows, rows), (0, 2, 1)).reshape(
        rows * rows, length // rows
    )

    place = {}
    for slot, (travels, _) in enumerate(PLAN):
        for part, key in enumerate(travels):
            place[key] = (slot, part, len(travels))
    buffers, arrived, kept = {}, {}, {}
    halves = [list(range(seq // 2)), list(range(seq // 2, seq))]
    sum_last, output = None, None

    def spot(key):
        slot, part, parts = place[key]
        return (part, parts), buffers.get(slot)

    def first(chunks):
        results = first_stage(chunks, [place[1, m][1:] for m in chunks], seq, x3, mix_first, twiddle)
        for m, sent in zip(chunks, results):
            buffers[place[1, m][0]] = sent

    first((0,))
    ups_first, ups_second, downs_first, downs_second, sum_first, *sums = prepare_stage(mine, weights)
    for slot, (travels, tasks) in enumerate(PLAN):
        done = exchange(buffers[slot])
        for part, key in enumerate(travels):
            arrived[key] = (done, part)
        for name, n in tasks:
            if name == FIRST:
                first(tuple(range(1, CHUNKS)))
            elif name == BACK:
                own, send = back_stage(g3, downs_second)
                back = (own, partner(send))
            elif name == SECOND:
                buffers[place[2, n][0]] = second_stage(w2t, arrived[1, n], *spot((2, n)), rows)
            elif name == HIDDEN:
                hidden, own, send = hidden_stage(n, x3, arrived[2, n], ups_first)
                kept[HIDDEN, n] = hidden
                kept[UP, n] = (own, partner(send))
            elif name == MIDDLE:
                down_own, down_send, grad_own, grad_send, *sums = middle_stage(
                    n, *kept[UP, n], *back, ups_second, downs_first, sums
                )
                kept[GRAD, n] = (grad_own, partner(grad_send))
                kept[DOWN, n] = (down_own, partner(down_send))
            elif name == INPUTS:
                buffers[place[3, n][0]], kept[BASE, n], sum_first = input_stage(
                    n,
                    x3,
                    g3,
                    arrived[2, n],
                    kept[HIDDEN, n],
                    *kept[GRAD, n],
                    ups_first,
                    sum_first,
                    *spot((3, n)),
                )
            elif name == OUTPUTS:
                output, sum_last = output_stage(n, g3, kept[HIDDEN, n], *kept[DOWN, n], downs_second, sum_last, output)
            elif name == FOURTH:
                buffers[place[4, n][0]] = second_stage(w2, arrived[3, n], *spot((4, n)), rows)

    width = up_first.shape[1]
    after = (buffers[place[4, CHUNKS - 1][0]], arrived[4, CHUNKS - 2][0])
    wholes = []
    for n, values in enumerate((sums, (sum_first, sum_last))):
        collected = collect_stage(1.0 / length, width, values)
        part = lax.psum_scatter(
            collected.reshape(-1, width), SEQ, scatter_dimension=0, axis_index_groups=halves, tiled=True
        )
        other = lax.ppermute(part, SEQ, [(d, (d + seq // 2) % seq) for d in range(seq)])
        other = tie(other, after[n])
        part = (part.astype(F32) + other.astype(F32)).astype(BF)
        whole = lax.all_gather(part, SEQ, axis=0, axis_index_groups=halves, tiled=True)
        wholes.append(whole.reshape(collected.shape))
    grads = finish_stage(mine, wholes, weights)
    tw_cols = tie(tw_cols, grads)
    fields = [arrived[4, n] for n in range(CHUNKS)]
    bases = [kept[BASE, n] for n in range(CHUNKS)]
    grad_inputs = last_stage(rows, length, mix_first, tw_cols, fields, bases)
    return (
        output.reshape(local_rows, channels),
        grad_inputs.reshape(local_rows, channels),
        *grads,
    )


def shards(*args):
    _, _, twiddle, _, up_first = args[:5]
    rows, length = twiddle.shape
    blocks, width = up_first.shape[0], up_first.shape[1]
    seq = length // rows
    fits = (
        blocks * (width // NBLK) == LANES
        and 2 * blocks == NBLK
        and rows == 16
        and seq == 16
        and length % (CHUNKS * seq) == 0
    )
    if fits:
        return chunked_shards(seq, *args)
    return general_shards(*args)


def solution(mesh):
    in_specs = (
        P(SEQ, FSDP),
        P(),
        P(SEQ, None),
        P(),
        P(FSDP, None, None),
        P(FSDP, None, None),
        P(FSDP, None, None),
        P(FSDP, None, None),
        P(SEQ, FSDP),
    )
    out_specs = (
        P(SEQ, FSDP),
        P(SEQ, FSDP),
        P(FSDP, None, None),
        P(FSDP, None, None),
        P(FSDP, None, None),
        P(FSDP, None, None),
    )
    return jax.shard_map(shards, mesh=mesh, in_specs=in_specs, out_specs=out_specs, check_vma=False)
```
